32 devices in a mesh: dp: 4 (over y, x), space: 8 (over z, core).
Axes of the slice: x: 2, y: 2, z: 4, core: 2. Of those that a mesh axis runs over, the one named last changes fastest.
Arguments:
- features: bfloat16 [4, 128, 64, 128], P('dp', 'space'), may hold values from -6 to 6
- weight_one: bfloat16 [27, 128, 128], replicated, may hold values from -0.125 to 0.125
- weight_two: bfloat16 [27, 128, 128], replicated, may hold values from -0.125 to 0.125
- cotangent: bfloat16 [4, 128, 64, 128], P('dp', 'space'), may hold values from -6 to 6
- brick_cell: int32 [4, 128], P('dp', 'space'), may hold values from 0 to 127, as said below
- voxel_mask: int32 [4, 128, 64], P('dp', 'space'), may hold values 0 or 1
Outputs:
- block_out: bfloat16 [4, 128, 64, 128], P('dp', 'space')
- input_grad: bfloat16 [4, 128, 64, 128], P('dp', 'space')
- weight_grad_one: float32 [442368], P(('dp', 'space'))
- weight_grad_two: float32 [442368], P(('dp', 'space'))
The draws below stay inside these ranges and needn't reach their ends.
Inputs may be any that keep to these rules, and one draw needn't show every extreme that they name: `brick_cell`: within one device's 16 entries of a scene the cells are distinct.
All inputs are finite; a program needn't handle non-finite values. No bound on the sum of `voxel_mask` on one device may be relied on, other than what follows from the above.
Results may differ from the reference program's by a relative error of at most 0.0052.
Values may be sent and summed in bfloat16 or wider, within the bound.
A program may use at most 128 MiB of HBM per device.

```python
import math
import jax
import jax.numpy as jnp
from jax import lax

CHANNELS = 128
BRICK_DEV = 16
LAYERS_X = 2
SIDE = 8
SCENES = 4
BRICKS = 128
N_SPACE = 8


def draw_brick_cell(key, part):
    positions = LAYERS_X * SIDE * SIDE
    blocks = SCENES * BRICKS // BRICK_DEV
    scores = jax.random.randint(key, (blocks, positions), 0, 1 << 20) * positions + jnp.arange(positions, dtype=jnp.int32)[None, :]
    chosen = jnp.argsort(scores, axis=1)[:, :BRICK_DEV]
    return chosen.astype(jnp.int32).reshape(SCENES, BRICKS)


def set_ends(drawn, key, low, largest):
    place = [jax.random.randint(jax.random.fold_in(key, axis), (), 0, length) for axis, length in enumerate(drawn.shape)]
    widest = drawn.shape.index(max(drawn.shape))
    beside = place[:widest] + [(place[widest] + 1) % drawn.shape[widest]] + place[widest + 1:]
    return drawn.at[tuple(place)].set(low).at[tuple(beside)].set(largest)


def steps_of(own_key, shape, cuts, least, largest):
    loudness = 1.0
    for dim, blocks in cuts:
        draws = jax.random.uniform(jax.random.fold_in(jax.random.fold_in(own_key, 6), dim), (blocks,), jnp.float32, least / len(cuts), largest / len(cuts))
        loudness = loudness * jnp.repeat(jnp.exp(draws), shape[dim] // blocks).reshape((-1,) + (1,) * (len(shape) - 1 - dim))
    return loudness


def noise(own_key, shape, deviation, limit, split=(), kind=jnp.bfloat16):
    drawn = deviation * jax.random.normal(own_key, shape, jnp.float32)
    if split:
        drawn = drawn * steps_of(own_key, shape, split, -0.22, 0.18)
    return jnp.clip(drawn, -limit, limit).astype(kind)


def setup_inputs(seed: int = 0) -> dict:
    keys = jax.random.split(jax.random.key(seed), 7)
    features = noise(keys[0], (SCENES, BRICKS, 64, CHANNELS), 1.0, 6.0, ((0, 4), (1, 8)))
    weight_one = noise(keys[1], (27, CHANNELS, CHANNELS), (27 * CHANNELS * 3 // 5) ** -0.5, 0.125)
    weight_two = noise(keys[2], (27, CHANNELS, CHANNELS), (27 * CHANNELS * 3 // 5) ** -0.5, 0.125)
    cotangent = noise(keys[3], (SCENES, BRICKS, 64, CHANNELS), 1.0, 6.0, ((0, 4), (1, 8)))
    brick_cell = draw_brick_cell(jax.random.fold_in(keys[6], 71), 0)
    voxel_mask = set_ends((jax.random.randint(keys[5], (SCENES, BRICKS, 64), 0, 5) < 3).astype(jnp.int32), jax.random.fold_in(keys[5], 1), 0, 1)
    return {"features": features, "weight_one": weight_one, "weight_two": weight_two, "cotangent": cotangent, "brick_cell": brick_cell, "voxel_mask": voxel_mask}


offset_list = [(shift_x, shift_y, shift_z) for shift_x in (-1, 0, 1) for shift_y in (-1, 0, 1) for shift_z in (-1, 0, 1)]

def take_layers(source, shift_step, along):
    if shift_step == -1:
        return lax.slice_in_dim(source, 3, 4, axis=along)
    if shift_step == 1:
        return lax.slice_in_dim(source, 0, 1, axis=along)
    return source

def gather_windows(extended, neighbours):
    slab_list = []
    for shift_x in (-1, 0, 1):
        columns = []
        for shift_y in (-1, 0, 1):
            pieces = []
            for shift_z in (-1, 0, 1):
                tap_index = (shift_x + 1) * 9 + (shift_y + 1) * 3 + shift_z + 1
                sliced = take_layers(take_layers(take_layers(extended, shift_x, 1), shift_y, 2), shift_z, 3)
                pieces.append(jnp.take(sliced, neighbours[:, tap_index], axis=0))
            columns.append(jnp.concatenate(pieces, axis=3))
        slab_list.append(jnp.concatenate(columns, axis=2))
    return jnp.concatenate(slab_list, axis=1)

def windows_of(values, neighbours):
    channels = values.shape[2]
    padding = jnp.zeros((1, 64, channels), values.dtype)
    extended = jnp.concatenate([values, padding], axis=0).reshape(-1, 4, 4, 4, channels)
    return gather_windows(extended, neighbours)

def apply_taps(windows, weight, mirrored):
    bricks = windows.shape[0]
    channels = windows.shape[-1]
    summed = jnp.zeros((bricks * 64, weight.shape[2]), jnp.float32)
    for tap_index, (shift_x, shift_y, shift_z) in enumerate(offset_list):
        if mirrored:
            start_x, start_y, start_z = (1 - shift_x, 1 - shift_y, 1 - shift_z)
        else:
            start_x, start_y, start_z = (1 + shift_x, 1 + shift_y, 1 + shift_z)
        window = windows[:, start_x:start_x + 4, start_y:start_y + 4, start_z:start_z + 4].reshape(bricks * 64, channels)
        if mirrored:
            summed = summed + lax.dot_general(window, weight[tap_index], (((1,), (1,)), ((), ())), preferred_element_type=jnp.float32)
        else:
            summed = summed + jnp.dot(window, weight[tap_index], preferred_element_type=jnp.float32)
    return summed.reshape(bricks, 64, -1)

def weight_taps(windows, gradient):
    bricks = windows.shape[0]
    channels = windows.shape[-1]
    grad_rows = gradient.reshape(bricks * 64, -1)
    collected = []
    for shift_x, shift_y, shift_z in offset_list:
        window = windows[:, 1 + shift_x:5 + shift_x, 1 + shift_y:5 + shift_y, 1 + shift_z:5 + shift_z].reshape(bricks * 64, channels)
        collected.append(lax.dot_general(window, grad_rows, (((0,), (0,)), ((), ())), preferred_element_type=jnp.float32))
    return jnp.stack(collected)

def silu_slope(values):
    logistic = jax.nn.sigmoid(values)
    return logistic * (1.0 + values * (1.0 - logistic))

def neighbour_table(cell_ids):
    bricks = cell_ids.shape[0]
    ordering = jnp.arange(bricks, dtype=jnp.int32)
    extent = N_SPACE * LAYERS_X
    layer_x = ordering // BRICK_DEV * LAYERS_X + cell_ids // (SIDE * SIDE)
    layer_y = cell_ids // SIDE % SIDE
    layer_z = cell_ids % SIDE
    lookup = jnp.full((extent, SIDE, SIDE), bricks, jnp.int32)
    lookup = lookup.at[layer_x, layer_y, layer_z].set(ordering)
    columns = []
    for shift_x, shift_y, shift_z in offset_list:
        target_x = layer_x + shift_x
        target_y = layer_y + shift_y
        target_z = layer_z + shift_z
        inside = (target_x >= 0) & (target_x < extent) & (target_y >= 0) & (target_y < SIDE) & (target_z >= 0) & (target_z < SIDE)
        located = lookup[jnp.clip(target_x, 0, extent - 1), jnp.clip(target_y, 0, SIDE - 1), jnp.clip(target_z, 0, SIDE - 1)]
        columns.append(jnp.where(inside, located, bricks).astype(jnp.int32))
    return jnp.stack(columns, axis=1)

def reference(features, weight_one, weight_two, cotangent, brick_cell, voxel_mask):
    outputs = []
    input_grads = []
    grad_one = jnp.zeros((27, CHANNELS, CHANNELS), jnp.float32)
    grad_two = jnp.zeros((27, CHANNELS, CHANNELS), jnp.float32)
    for scene_index in range(SCENES):
        neighbours = neighbour_table(brick_cell[scene_index])
        occupancy = voxel_mask[scene_index].astype(jnp.float32)[:, :, None]
        masked = (features[scene_index].astype(jnp.float32) * occupancy).astype(jnp.bfloat16)
        masked_windows = windows_of(masked, neighbours)
        first_act = apply_taps(masked_windows, weight_one, False) * occupancy
        hidden = jax.nn.silu(first_act).astype(jnp.bfloat16)
        hidden_windows = windows_of(hidden, neighbours)
        second_act = apply_taps(hidden_windows, weight_two, False) * occupancy
        residual_sum = masked.astype(jnp.float32) + second_act
        outputs.append(jax.nn.silu(residual_sum).astype(jnp.bfloat16))
        grad_out = (cotangent[scene_index].astype(jnp.float32) * occupancy * silu_slope(residual_sum)).astype(jnp.bfloat16)
        hidden_grad = apply_taps(windows_of(grad_out, neighbours), weight_two, True) * occupancy
        grad_mid = (hidden_grad * silu_slope(first_act)).astype(jnp.bfloat16)
        through = apply_taps(windows_of(grad_mid, neighbours), weight_one, True)
        input_grads.append(((grad_out.astype(jnp.float32) + through) * occupancy).astype(jnp.bfloat16))
        grad_two = grad_two + weight_taps(hidden_windows, grad_out)
        grad_one = grad_one + weight_taps(masked_windows, grad_mid)
    factor = 1.0 / math.sqrt(SCENES * BRICKS * 64)
    return (jnp.stack(outputs), jnp.stack(input_grads), (grad_one * factor).reshape(-1), (grad_two * factor).reshape(-1))
```

```python
import functools
import math

import jax
import jax.numpy as jnp
from jax import lax
from jax.experimental import pallas as pl
from jax.experimental.pallas import tpu as pltpu
from jax.sharding import PartitionSpec as P

LAYERS_X = 2
SIDE = 8
EDGE = 4
TAPS = 27
FAR = -1000000.0
MESH = pl.DeviceIdType.MESH
F32 = jnp.float32
BF16 = jnp.bfloat16
VMEM_LIMIT = 48 * 1024 * 1024

SPANS = {-1: (0, 1, 3, 4), 0: (1, 5, 0, 4), 1: (5, 6, 0, 1)}


def silu_slope(values):
    logistic = jax.nn.sigmoid(values)
    return logistic * (1.0 + values * (1.0 - logistic))


def kernel(
    n_dp, n_space, fused, factor,
    feat_hbm, cot_hbm, mask_hbm, cell_hbm, w1_hbm, w2_hbm,
    out_ref, grad_in_ref, g1_ref, g2_ref,
    feat_ref, cot_ref, mask_ref, cell_ref, w1_ref, w2_ref, load_sem,
    win_a, win_b, win_c, first, grad_out, g_t, occ, stage, stage_cot,
    send_low, send_high, from_low, from_high, cells, cells_low, cells_high,
    halo_send, halo_recv, cell_sem, *reduce_refs,
):
    bricks = mask_ref.shape[0]
    channels = feat_ref.shape[1]
    voxels = EDGE**3
    plane_rows = EDGE * EDGE * bricks
    dp = lax.axis_index("dp")
    space = lax.axis_index("space")
    has_low = space > 0
    has_high = space < n_space - 1
    low_id = (dp, lax.max(space - 1, 0))
    high_id = (dp, lax.min(space + 1, n_space - 1))
    core = space % 2
    depth = space // 2
    n_depth = n_space // 2

    core_id = (dp, depth * 2 + 1 - core)
    dp_ids = [((dp + j) % n_dp, space) for j in range(1, n_dp)]
    depth_ids = [(dp, (depth + j) % n_depth * 2 + core) for j in range(1, n_depth)]

    loads = [
        pltpu.make_async_copy(source, target, load_sem.at[index])
        for index, (source, target) in enumerate([
            (cell_hbm, cell_ref), (mask_hbm, mask_ref), (feat_hbm, feat_ref),
            (w1_hbm, w1_ref), (cot_hbm, cot_ref), (w2_hbm, w2_ref),
        ])
    ]
    for load in loads:
        load.start()

    barrier = pltpu.get_barrier_semaphore()

    @pl.when(has_low)
    def _():
        pl.semaphore_signal(barrier, inc=1, device_id=low_id, device_id_type=MESH)

    @pl.when(has_high)
    def _():
        pl.semaphore_signal(barrier, inc=1, device_id=high_id, device_id_type=MESH)

    expected = has_low.astype(jnp.int32) + has_high.astype(jnp.int32)
    if fused:
        for partner in dp_ids + depth_ids:
            pl.semaphore_signal(barrier, inc=1, device_id=partner, device_id_type=MESH)
        expected = expected + (n_dp + n_depth - 2)
    def halo_copies(phase):
        down = pltpu.make_async_remote_copy(
            src_ref=send_low.at[phase], dst_ref=from_high.at[phase],
            send_sem=halo_send.at[phase, 0], recv_sem=halo_recv.at[phase, 0],
            device_id=low_id, device_id_type=MESH,
        )
        up = pltpu.make_async_remote_copy(
            src_ref=send_high.at[phase], dst_ref=from_low.at[phase],
            send_sem=halo_send.at[phase, 1], recv_sem=halo_recv.at[phase, 1],
            device_id=high_id, device_id_type=MESH,
        )
        return down, up

    def cell_copies():
        down = pltpu.make_async_remote_copy(
            src_ref=cells, dst_ref=cells_high,
            send_sem=cell_sem.at[0], recv_sem=cell_sem.at[1],
            device_id=low_id, device_id_type=MESH,
        )
        up = pltpu.make_async_remote_copy(
            src_ref=cells, dst_ref=cells_low,
            send_sem=cell_sem.at[2], recv_sem=cell_sem.at[3],
            device_id=high_id, device_id_type=MESH,
        )
        return down, up

    def start_pair(down, up):
        @pl.when(has_low)
        def _():
            down.start()

        @pl.when(has_high)
        def _():
            up.start()

    def wait_pair(down, up):
        @pl.when(has_low)
        def _():
            down.wait_send()
            up.wait_recv()

        @pl.when(has_high)
        def _():
            up.wait_send()
            down.wait_recv()

    def send_halo(phase, win):
        send_low[phase] = win[1, 1:5, 1:5]
        send_high[phase] = win[4, 1:5, 1:5]
        start_pair(*halo_copies(phase))

    @pl.when(jnp.logical_not(has_low))
    def _():
        from_low[...] = jnp.zeros_like(from_low)
        cells_low[...] = jnp.zeros_like(cells_low)

    @pl.when(jnp.logical_not(has_high))
    def _():
        from_high[...] = jnp.zeros_like(from_high)
        cells_high[...] = jnp.zeros_like(cells_high)

    loads[0].wait()
    cell = cell_ref[...]
    key = (
        (cell // (SIDE * SIDE) + LAYERS_X) * 100 + (cell // SIDE % SIDE + 1) * 10 + cell % SIDE + 1
    ).astype(F32)
    square = (bricks, bricks)
    diagonal = lax.broadcasted_iota(jnp.int32, square, 0) == lax.broadcasted_iota(jnp.int32, square, 1)
    column = jnp.sum(
        jnp.where(diagonal, jnp.broadcast_to(key, square), 0.0), axis=1, keepdims=True
    )
    col_key = jnp.broadcast_to(column, (bricks, 128))
    brick = lax.broadcasted_iota(jnp.int32, (bricks, 128), 0)
    lane_of = lax.broadcasted_iota(jnp.int32, (bricks, 128), 1)
    own_row = jnp.sum(jnp.where(brick == lane_of, col_key, 0.0), axis=0, keepdims=True)
    beside_row = jnp.sum(jnp.where(brick + bricks == lane_of, col_key, 0.0), axis=0, keepdims=True)
    cells[...] = jnp.broadcast_to(beside_row, (8, 128))

    loads[1].wait()
    loads[2].wait()
    stage[...] = feat_ref[...].astype(F32)
    occupied = mask_ref[...].astype(F32)
    for voxel in range(voxels):
        x, y, z = voxel // 16, voxel // 4 % 4, voxel % 4
        kept = jnp.broadcast_to(occupied[:, voxel : voxel + 1], (bricks, channels))
        occ[x, y, z] = kept.astype(BF16)
        rows = stage[pl.ds(voxel, bricks, stride=voxels), :] * kept
        win_a[x + 1, y + 1, z + 1] = rows.astype(BF16)

    pl.semaphore_wait(barrier, expected)
    start_pair(*cell_copies())
    send_halo(0, win_a)

    lane = lax.broadcasted_iota(jnp.int32, (8, 128), 1)
    beside_lane = jnp.logical_and(lane >= bricks, lane < 2 * bricks)
    own_key = jnp.where(lane < bricks, jnp.broadcast_to(own_row, (8, 128)), FAR)
    layer_key = 100.0 * LAYERS_X
    def picker(row_key, shift_x, shift_y, shift_z):
        width = bricks if shift_x == 0 else 2 * bricks
        row_key = jnp.concatenate([row_key] * (bricks // 8), axis=0)
        wanted = col_key + float(shift_x * 100 + shift_y * 10 + shift_z)
        return jnp.where(wanted == row_key, 1.0, 0.0)[:, :width].astype(BF16)

    directions = [
        (x, y, z) for x in (0, -1, 1) for y in (-1, 0, 1) for z in (-1, 0, 1) if (x, y, z) != (0, 0, 0)
    ]
    pickers = {d: picker(own_key, *d) for d in directions if d[0] == 0}

    def fill(win, phase, which):
        for direction in directions:
            shift_x, shift_y, shift_z = direction
            if (shift_x == 0) != (which == 0):
                continue
            wx0, wx1, sx0, sx1 = SPANS[shift_x]
            wy0, wy1, sy0, sy1 = SPANS[shift_y]
            wz0, wz1, sz0, sz1 = SPANS[shift_z]
            source = win[sx0 + 1 : sx1 + 1, sy0 + 1 : sy1 + 1, sz0 + 1 : sz1 + 1]
            if shift_x != 0:
                halo = from_low if shift_x < 0 else from_high
                beside = halo[phase, sy0:sy1, sz0:sz1][None]
                source = jnp.concatenate([source, beside], axis=3)
            count = (sx1 - sx0) * (sy1 - sy0) * (sz1 - sz0)
            source = source.reshape(count, source.shape[3], channels)
            pick = pickers[direction]
            pick = jnp.broadcast_to(pick[None], (count,) + pick.shape)
            rows = lax.dot_general(
                pick, source, (((2,), (1,)), ((0,), (0,))), preferred_element_type=F32
            ).astype(BF16)
            win[wx0:wx1, wy0:wy1, wz0:wz1] = rows.reshape(
                wx1 - wx0, wy1 - wy0, wz1 - wz0, bricks, channels
            )

    def conv_planes(win, weight, planes, transposed):
        lefts, rights = [], []
        empty = jnp.zeros((channels, channels), BF16)
        for dx in range(3):
            for dy in range(3):
                for z in range(4):
                    rows = [
                        win[plane + dx, dy : dy + 4, z + 2 * half][:, None]
                        for plane in planes for half in range(2)
                    ]
                    rows = [
                        jnp.concatenate(rows[2 * p : 2 * p + 2], axis=1)[None]
                        for p in range(len(planes))
                    ]
                    rows = jnp.concatenate(rows, axis=0)
                    lefts.append(rows.reshape(len(planes) * 8 * bricks, channels))
                tap = 9 * dx + 3 * dy
                if transposed:
                    one, two, three = (weight[TAPS - 1 - tap - dz] for dz in range(3))
                else:
                    one, two, three = (weight[tap + dz] for dz in range(3))
                for pair in ((one, empty), (two, one), (three, two), (empty, three)):
                    rights.append(jnp.concatenate(pair, axis=0 if transposed else 1))
        left = jnp.concatenate(lefts, axis=1)
        right = jnp.concatenate(rights, axis=1 if transposed else 0)
        summed = lax.dot_general(
            left, right, (((1,), (1 if transposed else 0,)), ((), ())), preferred_element_type=F32
        )
        summed = summed.reshape(len(planes), EDGE, 2, bricks, 2 * channels)
        summed = jnp.stack([summed[..., :channels], summed[..., channels:]], axis=3)
        return summed.reshape(len(planes), EDGE, EDGE, bricks, channels)

    def over_planes(body, win, weight, planes, transposed=False):
        values = conv_planes(win, weight, planes, transposed)
        for index, plane in enumerate(planes):
            body(plane, values[index])

    def rows_of(plane, index):
        return pl.ds(plane * EDGE * EDGE + index, bricks, stride=voxels)

    def scatter_plane(plane, values):
        for index in range(EDGE * EDGE):
            stage[rows_of(plane, index), :] = values[index // EDGE, index % EDGE]

    def weight_grad(win, values, target, stops=((), (), ())):
        g_t[...] = values.reshape(EDGE * plane_rows, channels).T

        def step(dx, carry):
            pieces = [
                win[pl.ds(dx, 4), dy : dy + 4, dz : dz + 4].reshape(EDGE * plane_rows, channels)
                for dy in range(3) for dz in range(3)
            ]
            product = jnp.dot(
                g_t[...], jnp.concatenate(pieces, axis=1), preferred_element_type=F32
            )
            for tap in range(9):
                start = pl.multiple_of((dx * 9 + tap) * channels, channels)
                target[pl.ds(start, channels), :] = product[:, tap * channels : (tap + 1) * channels].T
            return carry

        for dx in range(3):
            lax.fori_loop(dx, dx + 1, step, 0)
            for after in stops[dx]:
                after()

    class Reduce:
        def __init__(self, refs, target):
            (self.total, self.own, self.send1, self.recv1, self.send2, self.recv2,
             self.send3, self.recv3, self.sems) = refs
            self.target = target

        def copies(self, phase):
            if phase == 2:
                base = 2 * n_dp
                return [
                    pltpu.make_async_remote_copy(
                        src_ref=self.send2.at[partner[0]], dst_ref=self.recv2.at[j],
                        send_sem=self.sems.at[base + 2 * j], recv_sem=self.sems.at[base + 2 * j + 1],
                        device_id=partner, device_id_type=MESH,
                    )
                    for j, partner in enumerate(dp_ids)
                ]
            base = 2 * n_dp + 2 * len(dp_ids)
            return [
                pltpu.make_async_remote_copy(
                    src_ref=self.send3.at[(depth + j + 1) % n_depth], dst_ref=self.recv3.at[j],
                    send_sem=self.sems.at[base + 2 * j], recv_sem=self.sems.at[base + 2 * j + 1],
                    device_id=partner, device_id_type=MESH,
                )
                for j, partner in enumerate(depth_ids)
            ]

        def start(self, phase):
            for copy in self.copies(phase):
                copy.start()

        def wait(self, phase):
            for copy in self.copies(phase):
                copy.wait()

        def core_copy(self, quarter):
            return pltpu.make_async_remote_copy(
                src_ref=self.send1.at[quarter], dst_ref=self.recv1.at[quarter],
                send_sem=self.sems.at[2 * quarter], recv_sem=self.sems.at[2 * quarter + 1],
                device_id=core_id, device_id_type=MESH,
            )

        def begin(self, low, high):
            rows = self.own.shape[2]

            def step(index, carry):
                block = self.total[pl.ds(pl.multiple_of(index * 2 * rows, 8), 2 * rows), :]
                one, two = block[:rows], block[rows:]
                self.own[index // n_depth, index % n_depth] = jnp.where(core == 0, one, two)
                theirs = jnp.where(core == 0, two, one)
                self.send1[index // n_depth, index % n_depth] = theirs.astype(BF16)
                return carry

            for quarter in range(low, high):
                lax.fori_loop(quarter * n_depth, (quarter + 1) * n_depth, step, 0)
                self.core_copy(quarter).start()

        def second(self, low, high):
            for quarter in range(low, high):
                self.core_copy(quarter).wait()
                summed = self.own[quarter] + self.recv1[quarter].astype(F32)
                self.own[quarter] = summed
                self.send2[quarter] = summed.astype(BF16)
                slot = (quarter - dp - 1 + n_dp) % n_dp

                @pl.when(dp != quarter)
                def _():
                    pltpu.make_async_remote_copy(
                        src_ref=self.send2.at[quarter], dst_ref=self.recv2.at[slot],
                        send_sem=self.sems.at[2 * n_dp + 2 * slot],
                        recv_sem=self.sems.at[2 * n_dp + 2 * slot + 1],
                        device_id=(quarter, space), device_id_type=MESH,
                    ).start()

        def third(self):
            self.wait(2)
            summed = self.own[dp]
            for j in range(n_dp - 1):
                summed = summed + self.recv2[j].astype(F32)
            self.own[0] = summed
            self.send3[...] = summed.astype(BF16)
            self.start(3)

        def finish(self):
            self.wait(3)
            summed = self.own[0, depth]
            for j in range(n_depth - 1):
                summed = summed + self.recv3[j].astype(F32)
            self.target[...] = summed * factor

    if fused:
        half = len(reduce_refs) // 2
        red2 = Reduce(reduce_refs[:half], g2_ref)
        red1 = Reduce(reduce_refs[half:], g1_ref)
        total_one, total_two = red1.total, red2.total
    else:
        total_one, total_two = g1_ref, g2_ref

    outer, inner = (0, EDGE - 1), tuple(range(1, EDGE - 1))
    fill(win_a, 0, 0)
    wait_pair(*cell_copies())
    low_key = jnp.where(
        jnp.logical_and(beside_lane, has_low), cells_low[...] - layer_key, own_key
    )
    high_key = jnp.where(
        jnp.logical_and(beside_lane, has_high), cells_high[...] + layer_key, own_key
    )

    for d in directions:
        if d[0] != 0:
            pickers[d] = picker(low_key if d[0] < 0 else high_key, *d)
    def first_plane(plane, values):
        values = values * occ[plane].astype(F32)
        first[plane] = values
        win_b[plane + 1, 1:5, 1:5] = (values * jax.nn.sigmoid(values)).astype(BF16)

    loads[3].wait()
    wait_pair(*halo_copies(0))
    fill(win_a, 0, 1)
    over_planes(first_plane, win_a, w1_ref, outer)
    send_halo(1, win_b)
    over_planes(first_plane, win_a, w1_ref, inner)
    loads[4].wait()
    stage_cot[...] = cot_ref[...].astype(F32)
    loads[5].wait()
    fill(win_b, 1, 0)

    def second_plane(plane, values):
        occupancy = occ[plane].astype(F32)
        total = win_a[plane + 1, 1:5, 1:5].astype(F32) + values * occupancy
        scatter_plane(plane, total * jax.nn.sigmoid(total))
        cot = jnp.stack([stage_cot[rows_of(plane, index), :] for index in range(EDGE * EDGE)])
        cot = cot.reshape(EDGE, EDGE, bricks, channels)
        gradient = (cot * occupancy * silu_slope(total)).astype(BF16)
        grad_out[plane] = gradient
        win_c[plane + 1, 1:5, 1:5] = gradient

    over_planes(second_plane, win_b, w2_ref, inner)
    wait_pair(*halo_copies(1))
    fill(win_b, 1, 1)
    over_planes(second_plane, win_b, w2_ref, outer)
    send_halo(2, win_c)
    out_ref[...] = stage[...].astype(BF16)

    def stops_of(reduce, early):
        ready = [-(-3 * (quarter + 1) // n_dp) - 1 for quarter in range(n_dp)]
        stops = [[], [], []]
        for quarter in range(n_dp):
            stops[ready[quarter]].append(functools.partial(reduce.begin, quarter, quarter + 1))
        if early:
            for quarter in range(early):
                stops[min(ready[quarter] + 1, 2)].append(
                    functools.partial(reduce.second, quarter, quarter + 1)
                )
        return stops

    half_way = n_dp // 2
    if fused:
        weight_grad(win_b, grad_out[...], total_two, stops_of(red2, 0))
    else:
        weight_grad(win_b, grad_out[...], total_two)
    def third_plane(plane, values):
        values = values * occ[plane].astype(F32)
        gradient = (values * silu_slope(first[plane])).astype(BF16)
        win_b[plane + 1, 1:5, 1:5] = gradient

    fill(win_c, 2, 0)
    over_planes(third_plane, win_c, w2_ref, inner, True)
    if fused:
        red2.second(0, half_way)
    wait_pair(*halo_copies(2))
    fill(win_c, 2, 1)
    over_planes(third_plane, win_c, w2_ref, outer, True)
    send_halo(3, win_b)
    if fused:
        red2.second(half_way, n_dp)
    if fused:
        weight_grad(win_a, win_b[1:5, 1:5, 1:5], total_one, stops_of(red1, half_way))
        red2.third()
    else:
        weight_grad(win_a, win_b[1:5, 1:5, 1:5], total_one)
    if fused:
        red1.second(half_way, n_dp)

    def fourth_plane(plane, values):
        values = grad_out[plane].astype(F32) + values
        scatter_plane(plane, values * occ[plane].astype(F32))

    fill(win_b, 3, 0)
    over_planes(fourth_plane, win_b, w1_ref, inner, True)
    wait_pair(*halo_copies(3))
    fill(win_b, 3, 1)
    over_planes(fourth_plane, win_b, w1_ref, outer, True)
    grad_in_ref[...] = stage[...].astype(BF16)
    if fused:
        red1.third()
        red2.finish()
        red1.finish()


def writer(*refs):
    count = len(refs) // 2
    sems = refs[-1]
    copies = [
        pltpu.make_async_copy(refs[index], refs[count + index], sems.at[index])
        for index in range(count)
    ]
    for copy in copies:
        copy.start()
    for copy in copies:
        copy.wait()


def shards(n_dp, n_space, features, weight_one, weight_two, cotangent, brick_cell, voxel_mask):
    bricks, channels = features.shape[1], features.shape[3]
    factor = 1.0 / math.sqrt(n_dp * n_space * bricks * 64)
    rows = TAPS * channels
    devices = n_dp * n_space
    fused = n_space % 2 == 0 and rows % devices == 0 and (rows // devices * 2) % 8 == 0
    cube = (EDGE, EDGE, EDGE, bricks, channels)
    flat = (bricks * EDGE**3, channels)
    window = (EDGE + 2, EDGE + 2, EDGE + 2, bricks, channels)
    plane = (EDGE, EDGE, bricks, channels)
    mask = voxel_mask[0]
    scratch = [
        pltpu.VMEM(flat, BF16), pltpu.VMEM(flat, BF16),
        pltpu.VMEM(mask.shape, jnp.int32), pltpu.VMEM(brick_cell.shape, jnp.int32),
        pltpu.VMEM(weight_one.shape, BF16), pltpu.VMEM(weight_two.shape, BF16),
        pltpu.SemaphoreType.DMA((6,)),
        pltpu.VMEM(window, BF16), pltpu.VMEM(window, BF16), pltpu.VMEM(window, BF16),
        pltpu.VMEM(cube, F32), pltpu.VMEM(cube, BF16),
        pltpu.VMEM((channels, EDGE**3 * bricks), BF16),
        pltpu.VMEM(cube, BF16), pltpu.VMEM(flat, F32), pltpu.VMEM(flat, F32),
        pltpu.VMEM((4,) + plane, BF16), pltpu.VMEM((4,) + plane, BF16),
        pltpu.VMEM((4,) + plane, BF16), pltpu.VMEM((4,) + plane, BF16),
        pltpu.VMEM((8, 128), F32), pltpu.VMEM((8, 128), F32), pltpu.VMEM((8, 128), F32),
        pltpu.SemaphoreType.DMA((4, 2)), pltpu.SemaphoreType.DMA((4, 2)),
        pltpu.SemaphoreType.DMA((4,)),
    ]
    if fused:
        part = rows // devices
        n_depth = n_space // 2
        for _ in range(2):
            scratch += [
                pltpu.VMEM((rows, channels), F32),
                pltpu.VMEM((n_dp, n_depth, part, channels), F32),
                pltpu.VMEM((n_dp, n_depth, part, channels), BF16),
                pltpu.VMEM((n_dp, n_depth, part, channels), BF16),
                pltpu.VMEM((n_dp, n_depth, part, channels), BF16),
                pltpu.VMEM((n_dp - 1, n_depth, part, channels), BF16),
                pltpu.VMEM((n_depth, part, channels), BF16),
                pltpu.VMEM((n_depth - 1, part, channels), BF16),
                pltpu.SemaphoreType.DMA((2 * n_dp + 2 * (n_dp - 1) + 2 * (n_depth - 1),)),
            ]
        grad_shape = (part, channels)
    else:
        grad_shape = (rows, channels)
    vmem = pl.BlockSpec(memory_space=pltpu.VMEM)
    hbm = pl.BlockSpec(memory_space=pltpu.HBM)
    results = pl.pallas_call(
        functools.partial(kernel, n_dp, n_space, fused, factor),
        out_shape=(
            jax.ShapeDtypeStruct(flat, BF16), jax.ShapeDtypeStruct(flat, BF16),
            jax.ShapeDtypeStruct(grad_shape, F32), jax.ShapeDtypeStruct(grad_shape, F32),
        ),
        in_specs=[hbm] * 6,
        out_specs=(vmem,) * 4,
        scratch_shapes=scratch,
        compiler_params=pltpu.CompilerParams(
            collective_id=0, has_side_effects=True, vmem_limit_bytes=VMEM_LIMIT
        ),
    )(*(
        pltpu.with_memory_space_constraint(argument, pltpu.HBM)
        for argument in (
            features.reshape(flat), cotangent.reshape(flat), mask, brick_cell,
            weight_one, weight_two,
        )
    ))

    if fused:
        results = pl.pallas_call(
            writer,
            out_shape=tuple(jax.ShapeDtypeStruct(r.shape, r.dtype) for r in results),
            in_specs=[vmem] * 4,
            out_specs=(hbm,) * 4,
            scratch_shapes=[pltpu.SemaphoreType.DMA((4,))],
            compiler_params=pltpu.CompilerParams(vmem_limit_bytes=1024 * 1024),
        )(*results)
    block_out, input_grad, grad_one, grad_two = results
    grad_one, grad_two = grad_one.reshape(-1), grad_two.reshape(-1)
    if not fused:
        grad_one, grad_two = (
            lax.psum_scatter(g, ("dp", "space"), scatter_dimension=0, tiled=True) * factor
            for g in (grad_one, grad_two)
        )
    shape = features.shape
    return (block_out.reshape(shape), input_grad.reshape(shape), grad_one, grad_two)


def solution(mesh):
    return jax.shard_map(
        functools.partial(shards, mesh.shape["dp"], mesh.shape["space"]),
        mesh=mesh,
        in_specs=(
            P("dp", "space", None, None),
            P(),
            P(),
            P("dp", "space", None, None),
            P("dp", "space"),
            P("dp", "space", None),
        ),
        out_specs=(
            P("dp", "space", None, None),
            P("dp", "space", None, None),
            P(("dp", "space")),
            P(("dp", "space")),
        ),
        check_vma=False,
    )
```

```python
import functools
import math

import jax
import jax.numpy as jnp
from jax import lax
from jax.experimental import pallas as pl
from jax.experimental.pallas import tpu as pltpu
from jax.sharding import PartitionSpec as P

LAYERS_X = 2
SIDE = 8
EDGE = 4
TAPS = 27
FAR = -1000000.0
MESH = pl.DeviceIdType.MESH
F32 = jnp.float32
BF16 = jnp.bfloat16
VMEM_LIMIT = 48 * 1024 * 1024

SPANS = {-1: (0, 1, 3, 4), 0: (1, 5, 0, 4), 1: (5, 6, 0, 1)}


def silu_slope(values):
    logistic = jax.nn.sigmoid(values)
    return logistic * (1.0 + values * (1.0 - logistic))


def kernel(
    n_dp, n_space, fused, factor,
    feat_hbm, cot_hbm, mask_hbm, cell_hbm, w1_hbm, w2_hbm,
    out_ref, grad_in_ref, g1_ref, g2_ref,
    feat_ref, cot_ref, mask_ref, cell_ref, w1_ref, w2_ref, load_sem,
    win_a, win_b, win_c, win_d, first, occ, stage, stage_cot, g_t,
    send_low, send_high, from_low, from_high, cells, cells_low, cells_high,
    halo_send, halo_recv, cell_sem, *reduce_refs,
):
    bricks = mask_ref.shape[0]
    channels = feat_ref.shape[1]
    voxels = EDGE**3
    plane_rows = EDGE * EDGE * bricks
    dp = lax.axis_index("dp")
    space = lax.axis_index("space")
    has_low = space > 0
    has_high = space < n_space - 1
    low_id = (dp, lax.max(space - 1, 0))
    high_id = (dp, lax.min(space + 1, n_space - 1))
    core = space % 2
    depth = space // 2
    n_depth = n_space // 2

    core_id = (dp, depth * 2 + 1 - core)
    dp_ids = [((dp + j) % n_dp, space) for j in range(1, n_dp)]
    space_ids = [(dp, (space + j) % n_space) for j in range(1, n_space)]

    loads = [
        pltpu.make_async_copy(source, target, load_sem.at[index])
        for index, (source, target) in enumerate([
            (cell_hbm, cell_ref), (mask_hbm, mask_ref), (feat_hbm, feat_ref),
            (w1_hbm, w1_ref), (cot_hbm, cot_ref), (w2_hbm, w2_ref),
        ])
    ]
    for load in loads:
        load.start()

    barrier = pltpu.get_barrier_semaphore()

    if fused:
        for partner in space_ids + dp_ids:
            pl.semaphore_signal(barrier, inc=1, device_id=partner, device_id_type=MESH)
        expected = n_space + n_dp - 2
    else:
        @pl.when(has_low)
        def _():
            pl.semaphore_signal(barrier, inc=1, device_id=low_id, device_id_type=MESH)

        @pl.when(has_high)
        def _():
            pl.semaphore_signal(barrier, inc=1, device_id=high_id, device_id_type=MESH)

        expected = has_low.astype(jnp.int32) + has_high.astype(jnp.int32)

    def halo_copies(phase):
        down = pltpu.make_async_remote_copy(
            src_ref=send_low.at[phase], dst_ref=from_high.at[phase],
            send_sem=halo_send.at[phase, 0], recv_sem=halo_recv.at[phase, 0],
            device_id=low_id, device_id_type=MESH,
        )
        up = pltpu.make_async_remote_copy(
            src_ref=send_high.at[phase], dst_ref=from_low.at[phase],
            send_sem=halo_send.at[phase, 1], recv_sem=halo_recv.at[phase, 1],
            device_id=high_id, device_id_type=MESH,
        )
        return down, up

    def cell_copies():
        down = pltpu.make_async_remote_copy(
            src_ref=cells, dst_ref=cells_high,
            send_sem=cell_sem.at[0], recv_sem=cell_sem.at[1],
            device_id=low_id, device_id_type=MESH,
        )
        up = pltpu.make_async_remote_copy(
            src_ref=cells, dst_ref=cells_low,
            send_sem=cell_sem.at[2], recv_sem=cell_sem.at[3],
            device_id=high_id, device_id_type=MESH,
        )
        return down, up

    def start_pair(down, up):
        @pl.when(has_low)
        def _():
            down.start()

        @pl.when(has_high)
        def _():
            up.start()

    def wait_pair(down, up):
        @pl.when(has_low)
        def _():
            down.wait_send()
            up.wait_recv()

        @pl.when(has_high)
        def _():
            up.wait_send()
            down.wait_recv()

    def send_halo(phase, win):
        send_low[phase] = win[1, 1:5, 1:5]
        send_high[phase] = win[4, 1:5, 1:5]
        start_pair(*halo_copies(phase))

    @pl.when(jnp.logical_not(has_low))
    def _():
        from_low[...] = jnp.zeros_like(from_low)
        cells_low[...] = jnp.zeros_like(cells_low)

    @pl.when(jnp.logical_not(has_high))
    def _():
        from_high[...] = jnp.zeros_like(from_high)
        cells_high[...] = jnp.zeros_like(cells_high)

    loads[0].wait()
    cell = cell_ref[...]
    key = (
        (cell // (SIDE * SIDE) + LAYERS_X) * 100 + (cell // SIDE % SIDE + 1) * 10 + cell % SIDE + 1
    ).astype(F32)
    square = (bricks, bricks)
    diagonal = lax.broadcasted_iota(jnp.int32, square, 0) == lax.broadcasted_iota(jnp.int32, square, 1)
    column = jnp.sum(
        jnp.where(diagonal, jnp.broadcast_to(key, square), 0.0), axis=1, keepdims=True
    )
    col_key = jnp.broadcast_to(column, (bricks, 128))
    brick = lax.broadcasted_iota(jnp.int32, (bricks, 128), 0)
    lane_of = lax.broadcasted_iota(jnp.int32, (bricks, 128), 1)
    own_row = jnp.sum(jnp.where(brick == lane_of, col_key, 0.0), axis=0, keepdims=True)
    beside_row = jnp.sum(jnp.where(brick + bricks == lane_of, col_key, 0.0), axis=0, keepdims=True)
    cells[...] = jnp.broadcast_to(beside_row, (8, 128))

    loads[1].wait()
    loads[2].wait()
    stage[...] = feat_ref[...].astype(F32)
    occupied = mask_ref[...].astype(F32)

    def place(planes):
        for x in planes:
            for y in range(EDGE):
                for z in range(EDGE):
                    voxel = (x * EDGE + y) * EDGE + z
                    kept = jnp.broadcast_to(occupied[:, voxel : voxel + 1], (bricks, channels))
                    occ[x, y, z] = kept.astype(BF16)
                    rows = stage[pl.ds(voxel, bricks, stride=voxels), :] * kept
                    win_a[x + 1, y + 1, z + 1] = rows.astype(BF16)

    outer, inner = (0, EDGE - 1), tuple(range(1, EDGE - 1))
    place(outer)
    pl.semaphore_wait(barrier, expected)
    start_pair(*cell_copies())
    send_halo(0, win_a)
    place(inner)

    lane = lax.broadcasted_iota(jnp.int32, (8, 128), 1)
    beside_lane = jnp.logical_and(lane >= bricks, lane < 2 * bricks)
    own_key = jnp.where(lane < bricks, jnp.broadcast_to(own_row, (8, 128)), FAR)
    layer_key = 100.0 * LAYERS_X
    def picker(row_key, shift_x, shift_y, shift_z):
        width = bricks if shift_x == 0 else 2 * bricks
        row_key = jnp.concatenate([row_key] * (bricks // 8), axis=0)
        wanted = col_key + float(shift_x * 100 + shift_y * 10 + shift_z)
        return jnp.where(wanted == row_key, 1.0, 0.0)[:, :width].astype(BF16)

    directions = [
        (x, y, z) for x in (0, -1, 1) for y in (-1, 0, 1) for z in (-1, 0, 1) if (x, y, z) != (0, 0, 0)
    ]
    pickers = {d: picker(own_key, *d) for d in directions if d[0] == 0}

    def fill(win, phase, which):
        for direction in directions:
            shift_x, shift_y, shift_z = direction
            if (shift_x == 0) != (which == 0):
                continue
            wx0, wx1, sx0, sx1 = SPANS[shift_x]
            wy0, wy1, sy0, sy1 = SPANS[shift_y]
            wz0, wz1, sz0, sz1 = SPANS[shift_z]
            source = win[sx0 + 1 : sx1 + 1, sy0 + 1 : sy1 + 1, sz0 + 1 : sz1 + 1]
            if shift_x != 0:
                halo = from_low if shift_x < 0 else from_high
                beside = halo[phase, sy0:sy1, sz0:sz1][None]
                source = jnp.concatenate([source, beside], axis=3)
            count = (sx1 - sx0) * (sy1 - sy0) * (sz1 - sz0)
            source = source.reshape(count, source.shape[3], channels)
            pick = pickers[direction]
            pick = jnp.broadcast_to(pick[None], (count,) + pick.shape)
            rows = lax.dot_general(
                pick, source, (((2,), (1,)), ((0,), (0,))), preferred_element_type=F32
            ).astype(BF16)
            win[wx0:wx1, wy0:wy1, wz0:wz1] = rows.reshape(
                wx1 - wx0, wy1 - wy0, wz1 - wz0, bricks, channels
            )

    def conv_planes(win, weight, planes, transposed):
        lefts, rights = [], []
        empty = jnp.zeros((channels, channels), BF16)
        for dx in range(3):
            for dy in range(3):
                for z in range(4):
                    rows = [
                        win[plane + dx, dy : dy + 4, z + 2 * half][:, None]
                        for plane in planes for half in range(2)
                    ]
                    rows = [
                        jnp.concatenate(rows[2 * p : 2 * p + 2], axis=1)[None]
                        for p in range(len(planes))
                    ]
                    rows = jnp.concatenate(rows, axis=0)
                    lefts.append(rows.reshape(len(planes) * 8 * bricks, channels))
                tap = 9 * dx + 3 * dy
                if transposed:
                    one, two, three = (weight[TAPS - 1 - tap - dz] for dz in range(3))
                else:
                    one, two, three = (weight[tap + dz] for dz in range(3))
                for pair in ((one, empty), (two, one), (three, two), (empty, three)):
                    rights.append(jnp.concatenate(pair, axis=0 if transposed else 1))
        left = jnp.concatenate(lefts, axis=1)
        right = jnp.concatenate(rights, axis=1 if transposed else 0)
        summed = lax.dot_general(
            left, right, (((1,), (1 if transposed else 0,)), ((), ())), preferred_element_type=F32
        )
        summed = summed.reshape(len(planes), EDGE, 2, bricks, 2 * channels)
        summed = jnp.stack([summed[..., :channels], summed[..., channels:]], axis=3)
        return summed.reshape(len(planes), EDGE, EDGE, bricks, channels)

    def over_planes(body, win, weight, planes, transposed=False):
        values = conv_planes(win, weight, planes, transposed)
        for index, plane in enumerate(planes):
            body(plane, values[index])

    def rows_of(plane, index):
        return pl.ds(plane * EDGE * EDGE + index, bricks, stride=voxels)

    def scatter_plane(plane, values):
        for index in range(EDGE * EDGE):
            stage[rows_of(plane, index), :] = values[index // EDGE, index % EDGE]

    def weight_grad(win, values, target):
        g_t[...] = values.T

        def step(dx, carry):
            pieces = [
                win[pl.ds(dx, 4), dy : dy + 4, dz : dz + 4].reshape(EDGE * plane_rows, channels)
                for dy in range(3) for dz in range(3)
            ]
            product = jnp.dot(
                g_t[...], jnp.concatenate(pieces, axis=1), preferred_element_type=F32
            )
            for tap in range(9):
                start = pl.multiple_of((dx * 9 + tap) * channels, channels)
                target[pl.ds(start, channels), :] = product[:, tap * channels : (tap + 1) * channels].T
            return carry

        lax.fori_loop(0, 3, step, 0)

    class Reduce:
        def __init__(self, refs, target):
            (self.total, self.own_t, self.other_t, self.other_win, self.send_b, self.recv_b,
             self.send_c, self.recv_c, self.own, self.pair_sem, self.send_b_sem, self.recv_b_sem,
             self.send_c_sem, self.recv_c_sem) = refs
            self.target = target
            self.part = self.own.shape[0]
            self.half = n_dp // 2
            self.receives = dp // self.half == core
            self.flip = depth // (n_depth // 2)

        def pair_copy(self, source, target, index):
            return pltpu.make_async_remote_copy(
                src_ref=source, dst_ref=target,
                send_sem=self.pair_sem.at[2 * index], recv_sem=self.pair_sem.at[2 * index + 1],
                device_id=core_id, device_id_type=MESH,
            )

        def win_copy(self, win):
            planes = pl.ds(1 - core, EDGE + 1)
            return self.pair_copy(win.at[planes], self.other_win.at[planes], 0)

        def win_wait(self, win):
            self.win_copy(win).wait()

        def grad_copy(self):
            return self.pair_copy(self.own_t, self.other_t, 1)

        def share_grad(self, values):
            self.own_t[...] = values.T
            self.grad_copy().start()

        def rows_at(self, block, z):
            start = (block * n_depth + z) * 2 * self.part + core * (channels // 2)
            return pl.ds(pl.multiple_of(start, 8), 2 * self.part)

        def b_copy(self, t, z):
            target = core * self.half + t
            slot = (dp - target - 1 + n_dp) % n_dp
            return pltpu.make_async_remote_copy(
                src_ref=self.send_b.at[t, z], dst_ref=self.recv_b.at[slot, z],
                send_sem=self.send_b_sem.at[t, z], recv_sem=self.recv_b_sem.at[slot, z],
                device_id=(target, space), device_id_type=MESH,
            )

        def b_arrival(self, j, z):
            return pltpu.make_async_remote_copy(
                src_ref=self.send_b.at[0, z], dst_ref=self.recv_b.at[j, z],
                send_sem=self.send_b_sem.at[0, z], recv_sem=self.recv_b_sem.at[j, z],
                device_id=dp_ids[j], device_id_type=MESH,
            )

        def send_chunk(self, t, z):
            block = self.total[self.rows_at(t, z), :]
            self.send_b[t, z, 0] = block[: self.part].astype(BF16)
            self.send_b[t, z, 1] = block[self.part :].astype(BF16)

            @pl.when(dp != core * self.half + t)
            def _():
                self.b_copy(t, z).start()

        def mirrored(self, index, count):
            return index + self.flip * (count - 1 - 2 * index)

        def depths(self):
            near = jnp.minimum(depth, n_depth - 1 - depth)
            order = list(range(n_depth - 1, n_depth // 2 - 1, -1))
            if n_depth == 4:
                order += [1 - near, near]
            else:
                order += list(range(n_depth // 2 - 1, -1, -1))
            return [self.mirrored(z, n_depth) for z in order]

        def multiply(self, win):
            groups = (TAPS + 1) // 4
            order = [3, 6, 2, 5, 1, 4, 0]
            depths = self.depths()
            waiting = [(t, n_depth - 1 - k) for k in range(n_depth) for t in range(self.half)]
            if n_depth == 4:
                needs = {1: (0, 2), 0: (0, 2)}
            else:
                needs = {}
            done = set()
            size = 2 * channels
            for group in order:
                corners = []
                for flip in range(2):
                    at = groups - 1 - group if flip else group
                    for side in range(2):
                        taps = [2 * at + index + side * (TAPS // 2) for index in range(2)]
                        corners.append([(tap // 9, tap // 3 % 3, tap % 3) for tap in taps])
                columns = []
                for index in range(2):
                    at = []
                    for axis in range(3):
                        a, b, c, d = (corner[index][axis] for corner in corners)
                        low = a + core * (b - a)
                        high = c + core * (d - c)
                        at.append(pl.ds(low + self.flip * (high - low), EDGE))
                    columns.append(jnp.concatenate(
                        [
                            w[tuple(at)].reshape(EDGE * plane_rows, channels)
                            for w in (win, self.other_win)
                        ],
                        axis=0,
                    ))
                both = jnp.concatenate([self.own_t[...], self.other_t[...]], axis=1)
                product = jnp.dot(
                    both, jnp.concatenate(columns, axis=1), preferred_element_type=F32
                )
                product = jnp.concatenate(
                    [product[:, :channels].T, product[:, channels:].T], axis=0
                )
                start = pl.multiple_of(self.mirrored(group, groups) * size, size)
                self.total[pl.ds(start, size), :] = product
                done.add(group)
                for t, z in list(waiting):
                    low, high = needs.get(z, (z, z + 1))
                    begin = (t * n_depth + low) * 2 * self.part
                    end = (t * n_depth + high) * 2 * self.part + channels // 2
                    if all(g in done for g in range(begin // size, -(-end // size))):
                        waiting.remove((t, z))
                        self.send_chunk(self.mirrored(t, self.half), depths[n_depth - 1 - z])

        def c_copy(self, z, side):
            slot = (depth - z - 1 + n_depth) % n_depth
            return pltpu.make_async_remote_copy(
                src_ref=self.send_c.at[z, side], dst_ref=self.recv_c.at[slot],
                send_sem=self.send_c_sem.at[z, side], recv_sem=self.recv_c_sem.at[slot],
                device_id=(dp, z * 2 + side), device_id_type=MESH,
            )

        def c_arrival(self, slot):
            return pltpu.make_async_remote_copy(
                src_ref=self.send_c.at[0, 0], dst_ref=self.recv_c.at[slot],
                send_sem=self.send_c_sem.at[0, 0], recv_sem=self.recv_c_sem.at[slot],
                device_id=core_id, device_id_type=MESH,
            )

        def forward(self, low, high):
            @pl.when(self.receives)
            def _():
                for z in self.depths()[low:high]:
                    for j in range(n_dp - 1):
                        self.b_arrival(j, z).wait_recv()
                    block = self.total[self.rows_at(dp - core * self.half, z), :]
                    sums = []
                    for side in range(2):
                        summed = block[side * self.part : (side + 1) * self.part]
                        for j in range(n_dp - 1):
                            summed = summed + self.recv_b[j, z, side].astype(F32)
                        sums.append(summed)
                        self.send_c[z, side] = summed.astype(BF16)

                        @pl.when(jnp.logical_or(z != depth, core != side))
                        def _():
                            self.c_copy(z, side).start()

                    @pl.when(z == depth)
                    def _():
                        self.own[...] = jnp.where(core == 0, sums[0], sums[1])

        def finish(self):
            @pl.when(jnp.logical_not(self.receives))
            def _():
                self.c_arrival(n_depth - 1).wait_recv()
                self.own[...] = self.recv_c[n_depth - 1].astype(F32)

            summed = self.own[...]
            for slot in range(n_depth - 1):
                self.c_arrival(slot).wait_recv()
                summed = summed + self.recv_c[slot].astype(F32)
            self.target[...] = summed * factor

        def drain(self):
            for t in range(self.half):
                @pl.when(dp != core * self.half + t)
                def _():
                    for z in range(n_depth):
                        self.b_copy(t, z).wait_send()

            @pl.when(self.receives)
            def _():
                for z in range(n_depth):
                    for side in range(2):
                        @pl.when(jnp.logical_or(z != depth, core != side))
                        def _():
                            self.c_copy(z, side).wait_send()

    if fused:
        count = len(reduce_refs) // 2
        red2 = Reduce(reduce_refs[:count], g2_ref)
        red1 = Reduce(reduce_refs[count:], g1_ref)

    def flat_of(win):
        return win[1:5, 1:5, 1:5].reshape(EDGE * plane_rows, channels)

    fill(win_a, 0, 0)
    wait_pair(*cell_copies())
    low_key = jnp.where(
        jnp.logical_and(beside_lane, has_low), cells_low[...] - layer_key, own_key
    )
    high_key = jnp.where(
        jnp.logical_and(beside_lane, has_high), cells_high[...] + layer_key, own_key
    )

    for d in directions:
        if d[0] != 0:
            pickers[d] = picker(low_key if d[0] < 0 else high_key, *d)
    def first_plane(plane, values):
        values = values * occ[plane].astype(F32)
        first[plane] = values
        win_b[plane + 1, 1:5, 1:5] = (values * jax.nn.sigmoid(values)).astype(BF16)

    loads[3].wait()
    wait_pair(*halo_copies(0))
    fill(win_a, 0, 1)
    if fused:
        red1.win_copy(win_a).start()
    over_planes(first_plane, win_a, w1_ref, outer)
    send_halo(1, win_b)
    over_planes(first_plane, win_a, w1_ref, inner)
    loads[4].wait()
    stage_cot[...] = cot_ref[...].astype(F32)
    loads[5].wait()
    fill(win_b, 1, 0)

    def second_plane(plane, values):
        occupancy = occ[plane].astype(F32)
        total = win_a[plane + 1, 1:5, 1:5].astype(F32) + values * occupancy
        scatter_plane(plane, total * jax.nn.sigmoid(total))
        cot = jnp.stack([stage_cot[rows_of(plane, index), :] for index in range(EDGE * EDGE)])
        cot = cot.reshape(EDGE, EDGE, bricks, channels)
        gradient = (cot * occupancy * silu_slope(total)).astype(BF16)
        win_c[plane + 1, 1:5, 1:5] = gradient

    over_planes(second_plane, win_b, w2_ref, inner)
    wait_pair(*halo_copies(1))
    fill(win_b, 1, 1)
    if fused:
        red2.win_copy(win_b).start()
    over_planes(second_plane, win_b, w2_ref, outer)
    send_halo(2, win_c)
    out_ref[...] = stage[...].astype(BF16)

    if fused:
        red2.share_grad(flat_of(win_c))
    else:
        weight_grad(win_b, flat_of(win_c), g2_ref)

    def third_plane(plane, values):
        values = values * occ[plane].astype(F32)
        gradient = (values * silu_slope(first[plane])).astype(BF16)
        win_d[plane + 1, 1:5, 1:5] = gradient

    fill(win_c, 2, 0)
    over_planes(third_plane, win_c, w2_ref, inner, True)
    if fused:
        red2.win_wait(win_b)
        red2.grad_copy().wait()
        red2.multiply(win_b)
    wait_pair(*halo_copies(2))
    fill(win_c, 2, 1)
    over_planes(third_plane, win_c, w2_ref, outer, True)
    send_halo(3, win_d)
    if fused:
        red1.share_grad(flat_of(win_d))
    else:
        weight_grad(win_a, flat_of(win_d), g1_ref)

    def fourth_plane(plane, values):
        values = win_c[plane + 1, 1:5, 1:5].astype(F32) + values
        scatter_plane(plane, values * occ[plane].astype(F32))

    fill(win_d, 3, 0)
    over_planes(fourth_plane, win_d, w1_ref, inner, True)
    if fused:
        red1.win_wait(win_a)
        red1.grad_copy().wait()
        red2.forward(0, 1)
        red1.multiply(win_a)
        red2.forward(1, n_depth - 1)
    wait_pair(*halo_copies(3))
    fill(win_d, 3, 1)
    over_planes(fourth_plane, win_d, w1_ref, outer, True)
    if fused:
        red2.forward(n_depth - 1, n_depth)
    grad_in_ref[...] = stage[...].astype(BF16)
    if fused:
        red1.forward(0, n_depth - 1)
        red2.finish()
        red1.forward(n_depth - 1, n_depth)
        red1.finish()
        red2.drain()
        red1.drain()


def writer(*refs):
    count = len(refs) // 2
    sems = refs[-1]
    copies = [
        pltpu.make_async_copy(refs[index], refs[count + index], sems.at[index])
        for index in range(count)
    ]
    for copy in copies:
        copy.start()
    for copy in copies:
        copy.wait()


def shards(n_dp, n_space, features, weight_one, weight_two, cotangent, brick_cell, voxel_mask):
    bricks, channels = features.shape[1], features.shape[3]
    factor = 1.0 / math.sqrt(n_dp * n_space * bricks * 64)
    rows = TAPS * channels
    devices = n_dp * n_space
    fused = (
        n_space % 2 == 0 and n_dp % 2 == 0 and rows % devices == 0
        and (rows // devices * 2) % 8 == 0
    )
    cube = (EDGE, EDGE, EDGE, bricks, channels)
    flat = (bricks * EDGE**3, channels)
    window = (EDGE + 2, EDGE + 2, EDGE + 2, bricks, channels)
    plane = (EDGE, EDGE, bricks, channels)
    mask = voxel_mask[0]
    scratch = [
        pltpu.VMEM(flat, BF16), pltpu.VMEM(flat, BF16),
        pltpu.VMEM(mask.shape, jnp.int32), pltpu.VMEM(brick_cell.shape, jnp.int32),
        pltpu.VMEM(weight_one.shape, BF16), pltpu.VMEM(weight_two.shape, BF16),
        pltpu.SemaphoreType.DMA((6,)),
        pltpu.VMEM(window, BF16), pltpu.VMEM(window, BF16),
        pltpu.VMEM(window, BF16), pltpu.VMEM(window, BF16),
        pltpu.VMEM(cube, F32), pltpu.VMEM(cube, BF16), pltpu.VMEM(flat, F32), pltpu.VMEM(flat, F32),
        pltpu.VMEM((channels, flat[0]), BF16),
        pltpu.VMEM((4,) + plane, BF16), pltpu.VMEM((4,) + plane, BF16),
        pltpu.VMEM((4,) + plane, BF16), pltpu.VMEM((4,) + plane, BF16),
        pltpu.VMEM((8, 128), F32), pltpu.VMEM((8, 128), F32), pltpu.VMEM((8, 128), F32),
        pltpu.SemaphoreType.DMA((4, 2)), pltpu.SemaphoreType.DMA((4, 2)),
        pltpu.SemaphoreType.DMA((4,)),
    ]
    if fused:
        part = rows // devices
        n_depth = n_space // 2
        half = n_dp // 2
        for _ in range(2):
            scratch += [
                pltpu.VMEM(((TAPS + 1) // 2 * channels, channels), F32),
                pltpu.VMEM((channels, flat[0]), BF16), pltpu.VMEM((channels, flat[0]), BF16),
                pltpu.VMEM(window, BF16),
                pltpu.VMEM((half, n_depth, 2, part, channels), BF16),
                pltpu.VMEM((n_dp - 1, n_depth, 2, part, channels), BF16),
                pltpu.VMEM((n_depth, 2, part, channels), BF16),
                pltpu.VMEM((n_depth, part, channels), BF16),
                pltpu.VMEM((part, channels), F32),
                pltpu.SemaphoreType.DMA((4,)),
                pltpu.SemaphoreType.DMA((half, n_depth)),
                pltpu.SemaphoreType.DMA((n_dp - 1, n_depth)),
                pltpu.SemaphoreType.DMA((n_depth, 2)),
                pltpu.SemaphoreType.DMA((n_depth,)),
            ]
        grad_shape = (part, channels)
    else:
        grad_shape = (rows, channels)
    vmem = pl.BlockSpec(memory_space=pltpu.VMEM)
    hbm = pl.BlockSpec(memory_space=pltpu.HBM)
    results = pl.pallas_call(
        functools.partial(kernel, n_dp, n_space, fused, factor),
        out_shape=(
            jax.ShapeDtypeStruct(flat, BF16), jax.ShapeDtypeStruct(flat, BF16),
            jax.ShapeDtypeStruct(grad_shape, F32), jax.ShapeDtypeStruct(grad_shape, F32),
        ),
        in_specs=[hbm] * 6,
        out_specs=(vmem,) * 4,
        scratch_shapes=scratch,
        compiler_params=pltpu.CompilerParams(
            collective_id=0, has_side_effects=True, vmem_limit_bytes=VMEM_LIMIT
        ),
    )(*(
        pltpu.with_memory_space_constraint(argument, pltpu.HBM)
        for argument in (
            features.reshape(flat), cotangent.reshape(flat), mask, brick_cell,
            weight_one, weight_two,
        )
    ))

    if fused:
        results = pl.pallas_call(
            writer,
            out_shape=tuple(jax.ShapeDtypeStruct(r.shape, r.dtype) for r in results),
            in_specs=[vmem] * 4,
            out_specs=(hbm,) * 4,
            scratch_shapes=[pltpu.SemaphoreType.DMA((4,))],
            compiler_params=pltpu.CompilerParams(vmem_limit_bytes=1024 * 1024),
        )(*results)
    block_out, input_grad, grad_one, grad_two = results
    grad_one, grad_two = grad_one.reshape(-1), grad_two.reshape(-1)
    if not fused:
        grad_one, grad_two = (
            lax.psum_scatter(g, ("dp", "space"), scatter_dimension=0, tiled=True) * factor
            for g in (grad_one, grad_two)
        )
    shape = features.shape
    return (block_out.reshape(shape), input_grad.reshape(shape), grad_one, grad_two)


def solution(mesh):
    return jax.shard_map(
        functools.partial(shards, mesh.shape["dp"], mesh.shape["space"]),
        mesh=mesh,
        in_specs=(
            P("dp", "space", None, None),
            P(),
            P(),
            P("dp", "space", None, None),
            P("dp", "space"),
            P("dp", "space", None),
        ),
        out_specs=(
            P("dp", "space", None, None),
            P("dp", "space", None, None),
            P(("dp", "space")),
            P(("dp", "space")),
        ),
        check_vma=False,
    )
```

```python
import functools
import math

import jax
import jax.numpy as jnp
from jax import lax
from jax.experimental import pallas as pl
from jax.experimental.pallas import tpu as pltpu
from jax.sharding import PartitionSpec as P

LAYERS_X = 2
SIDE = 8
EDGE = 4
TAPS = 27
FAR = -1000000.0
MESH = pl.DeviceIdType.MESH
F32 = jnp.float32
BF16 = jnp.bfloat16
VMEM_LIMIT = 48 * 1024 * 1024

SPANS = {-1: (0, 1, 3, 4), 0: (1, 5, 0, 4), 1: (5, 6, 0, 1)}


def silu_slope(values):
    logistic = jax.nn.sigmoid(values)
    return logistic * (1.0 + values * (1.0 - logistic))


def kernel(
    n_dp, n_space, fused, factor,
    feat_hbm, cot_hbm, mask_hbm, cell_hbm, w1_hbm, w2_hbm,
    out_ref, grad_in_ref, g1_ref, g2_ref,
    feat_ref, cot_ref, mask_ref, cell_ref, w1_ref, w2_ref, load_sem,
    win_a, win_b, win_c, win_d, first, resid, sums, occ, cot_cube, stage, stage_cot, g_t,
    send_low, send_high, from_low, from_high, cells, cells_low, cells_high,
    halo_send, halo_recv, cell_sem, *reduce_refs,
):
    bricks = mask_ref.shape[0]
    channels = feat_ref.shape[1]
    voxels = EDGE**3
    plane_rows = EDGE * EDGE * bricks
    dp = lax.axis_index("dp")
    space = lax.axis_index("space")
    has_low = space > 0
    has_high = space < n_space - 1
    low_id = (dp, lax.max(space - 1, 0))
    high_id = (dp, lax.min(space + 1, n_space - 1))
    core = space % 2
    depth = space // 2
    n_depth = n_space // 2

    core_id = (dp, depth * 2 + 1 - core)
    dp_ids = [((dp + j) % n_dp, space) for j in range(1, n_dp)]
    space_ids = [(dp, (space + j) % n_space) for j in range(1, n_space)]
    cross_ids = [((dp + j) % n_dp, core_id[1]) for j in range(1, n_dp)]

    loads = [
        pltpu.make_async_copy(source, target, load_sem.at[index])
        for index, (source, target) in enumerate([
            (cell_hbm, cell_ref), (mask_hbm, mask_ref), (feat_hbm, feat_ref),
            (w1_hbm, w1_ref), (cot_hbm, cot_ref), (w2_hbm, w2_ref),
        ])
    ]
    for load in loads:
        load.start()

    barrier = pltpu.get_barrier_semaphore()

    if fused:
        for partner in space_ids + dp_ids + cross_ids:
            pl.semaphore_signal(barrier, inc=1, device_id=partner, device_id_type=MESH)
        expected = n_space + 2 * n_dp - 3
    else:
        @pl.when(has_low)
        def _():
            pl.semaphore_signal(barrier, inc=1, device_id=low_id, device_id_type=MESH)

        @pl.when(has_high)
        def _():
            pl.semaphore_signal(barrier, inc=1, device_id=high_id, device_id_type=MESH)

        expected = has_low.astype(jnp.int32) + has_high.astype(jnp.int32)

    def halo_copies(phase):
        down = pltpu.make_async_remote_copy(
            src_ref=send_low.at[phase], dst_ref=from_high.at[phase],
            send_sem=halo_send.at[phase, 0], recv_sem=halo_recv.at[phase, 0],
            device_id=low_id, device_id_type=MESH,
        )
        up = pltpu.make_async_remote_copy(
            src_ref=send_high.at[phase], dst_ref=from_low.at[phase],
            send_sem=halo_send.at[phase, 1], recv_sem=halo_recv.at[phase, 1],
            device_id=high_id, device_id_type=MESH,
        )
        return down, up

    def cell_copies():
        down = pltpu.make_async_remote_copy(
            src_ref=cells, dst_ref=cells_high,
            send_sem=cell_sem.at[0], recv_sem=cell_sem.at[1],
            device_id=low_id, device_id_type=MESH,
        )
        up = pltpu.make_async_remote_copy(
            src_ref=cells, dst_ref=cells_low,
            send_sem=cell_sem.at[2], recv_sem=cell_sem.at[3],
            device_id=high_id, device_id_type=MESH,
        )
        return down, up

    def start_pair(down, up):
        @pl.when(has_low)
        def _():
            down.start()

        @pl.when(has_high)
        def _():
            up.start()

    def wait_pair(down, up):
        @pl.when(has_low)
        def _():
            down.wait_send()
            up.wait_recv()

        @pl.when(has_high)
        def _():
            up.wait_send()
            down.wait_recv()

    def send_halo(phase, win):
        send_low[phase] = win[1, 1:5, 1:5]
        send_high[phase] = win[4, 1:5, 1:5]
        start_pair(*halo_copies(phase))

    @pl.when(jnp.logical_not(has_low))
    def _():
        from_low[...] = jnp.zeros_like(from_low)
        cells_low[...] = jnp.zeros_like(cells_low)

    @pl.when(jnp.logical_not(has_high))
    def _():
        from_high[...] = jnp.zeros_like(from_high)
        cells_high[...] = jnp.zeros_like(cells_high)

    loads[0].wait()
    cell = cell_ref[...]
    key = (
        (cell // (SIDE * SIDE) + LAYERS_X) * 100 + (cell // SIDE % SIDE + 1) * 10 + cell % SIDE + 1
    ).astype(F32)
    square = (bricks, bricks)
    diagonal = lax.broadcasted_iota(jnp.int32, square, 0) == lax.broadcasted_iota(jnp.int32, square, 1)
    column = jnp.sum(
        jnp.where(diagonal, jnp.broadcast_to(key, square), 0.0), axis=1, keepdims=True
    )
    col_key = jnp.broadcast_to(column, (bricks, 128))
    brick = lax.broadcasted_iota(jnp.int32, (bricks, 128), 0)
    lane_of = lax.broadcasted_iota(jnp.int32, (bricks, 128), 1)
    own_row = jnp.sum(jnp.where(brick == lane_of, col_key, 0.0), axis=0, keepdims=True)
    beside_row = jnp.sum(jnp.where(brick + bricks == lane_of, col_key, 0.0), axis=0, keepdims=True)
    cells[...] = jnp.broadcast_to(beside_row, (8, 128))

    loads[1].wait()
    loads[2].wait()
    stage[...] = feat_ref[...].astype(F32)
    occupied = mask_ref[...].astype(F32)

    def place(planes):
        for x in planes:
            for y in range(EDGE):
                for z in range(EDGE):
                    voxel = (x * EDGE + y) * EDGE + z
                    kept = jnp.broadcast_to(occupied[:, voxel : voxel + 1], (bricks, channels))
                    occ[x, y, z] = kept.astype(BF16)
                    rows = stage[pl.ds(voxel, bricks, stride=voxels), :] * kept
                    win_a[x + 1, y + 1, z + 1] = rows.astype(BF16)

    outer, inner = (0, EDGE - 1), tuple(range(1, EDGE - 1))
    place(outer)
    pl.semaphore_wait(barrier, expected)
    start_pair(*cell_copies())
    send_halo(0, win_a)
    place(inner)

    lane = lax.broadcasted_iota(jnp.int32, (8, 128), 1)
    beside_lane = jnp.logical_and(lane >= bricks, lane < 2 * bricks)
    own_key = jnp.where(lane < bricks, jnp.broadcast_to(own_row, (8, 128)), FAR)
    layer_key = 100.0 * LAYERS_X
    def picker(row_key, shift_x, shift_y, shift_z):
        width = bricks if shift_x == 0 else 2 * bricks
        row_key = jnp.concatenate([row_key] * (bricks // 8), axis=0)
        wanted = col_key + float(shift_x * 100 + shift_y * 10 + shift_z)
        return jnp.where(wanted == row_key, 1.0, 0.0)[:, :width].astype(BF16)

    directions = [
        (x, y, z) for x in (0, -1, 1) for y in (-1, 0, 1) for z in (-1, 0, 1) if (x, y, z) != (0, 0, 0)
    ]
    pickers = {d: picker(own_key, *d) for d in directions if d[0] == 0}

    def fill(win, phase, which):
        for direction in directions:
            shift_x, shift_y, shift_z = direction
            if (shift_x == 0) != (which == 0):
                continue
            wx0, wx1, sx0, sx1 = SPANS[shift_x]
            wy0, wy1, sy0, sy1 = SPANS[shift_y]
            wz0, wz1, sz0, sz1 = SPANS[shift_z]
            source = win[sx0 + 1 : sx1 + 1, sy0 + 1 : sy1 + 1, sz0 + 1 : sz1 + 1]
            if shift_x != 0:
                halo = from_low if shift_x < 0 else from_high
                beside = halo[phase, sy0:sy1, sz0:sz1][None]
                source = jnp.concatenate([source, beside], axis=3)
            count = (sx1 - sx0) * (sy1 - sy0) * (sz1 - sz0)
            source = source.reshape(count, source.shape[3], channels)
            pick = pickers[direction]
            pick = jnp.broadcast_to(pick[None], (count,) + pick.shape)
            rows = lax.dot_general(
                pick, source, (((2,), (1,)), ((0,), (0,))), preferred_element_type=F32
            ).astype(BF16)
            win[wx0:wx1, wy0:wy1, wz0:wz1] = rows.reshape(
                wx1 - wx0, wy1 - wy0, wz1 - wz0, bricks, channels
            )

    def conv_rows(win, weight, planes, transposed, steps=(0, 1, 2)):
        lefts, rights = [], []
        empty = jnp.zeros((channels, channels), BF16)
        for dx in steps:
            for dy in range(3):
                for z in range(4):
                    rows = [
                        win[plane + dx, dy : dy + 4, z + 2 * half][:, None]
                        for plane in planes for half in range(2)
                    ]
                    rows = [
                        jnp.concatenate(rows[2 * p : 2 * p + 2], axis=1)[None]
                        for p in range(len(planes))
                    ]
                    rows = jnp.concatenate(rows, axis=0)
                    lefts.append(rows.reshape(len(planes) * 8 * bricks, channels))
                tap = 9 * dx + 3 * dy
                if transposed:
                    one, two, three = (weight[TAPS - 1 - tap - dz] for dz in range(3))
                else:
                    one, two, three = (weight[tap + dz] for dz in range(3))
                for pair in ((one, empty), (two, one), (three, two), (empty, three)):
                    rights.append(jnp.concatenate(pair, axis=0 if transposed else 1))
        left = jnp.concatenate(lefts, axis=1)
        right = jnp.concatenate(rights, axis=1 if transposed else 0)
        summed = lax.dot_general(
            left, right, (((1,), (1 if transposed else 0,)), ((), ())), preferred_element_type=F32
        )
        return summed.reshape(len(planes), 8 * bricks, 2 * channels)

    def as_plane(summed):
        summed = summed.reshape(EDGE, 2, bricks, 2 * channels)
        summed = jnp.stack([summed[..., :channels], summed[..., channels:]], axis=2)
        return summed.reshape(EDGE, EDGE, bricks, channels)

    def over_planes(body, win, weight, planes, transposed=False):
        values = conv_rows(win, weight, planes, transposed)
        for index, plane in enumerate(planes):
            body(plane, as_plane(values[index]))

    def inside(win, weight):
        sums[...] = conv_rows(win, weight, range(EDGE), False, (1,))
        sums[: EDGE - 1] += conv_rows(win, weight, range(EDGE - 1), False, (2,))
        sums[1:] += conv_rows(win, weight, range(1, EDGE), False, (0,))

    def across(win, weight):
        sums[:1] += conv_rows(win, weight, (0,), False, (0,))
        sums[EDGE - 1 :] += conv_rows(win, weight, (EDGE - 1,), False, (2,))

    def summed_planes(body, planes):
        for plane in planes:
            body(plane, as_plane(sums[plane]))

    def rows_of(plane, index):
        return pl.ds(plane * EDGE * EDGE + index, bricks, stride=voxels)

    def scatter_plane(target, plane, values):
        for index in range(EDGE * EDGE):
            target[rows_of(plane, index), :] = values[index // EDGE, index % EDGE]

    def weight_grad(win, values, target):
        g_t[...] = values.T

        def step(dx, carry):
            pieces = [
                win[pl.ds(dx, 4), dy : dy + 4, dz : dz + 4].reshape(EDGE * plane_rows, channels)
                for dy in range(3) for dz in range(3)
            ]
            product = jnp.dot(
                g_t[...], jnp.concatenate(pieces, axis=1), preferred_element_type=F32
            )
            for tap in range(9):
                start = pl.multiple_of((dx * 9 + tap) * channels, channels)
                target[pl.ds(start, channels), :] = product[:, tap * channels : (tap + 1) * channels].T
            return carry

        lax.fori_loop(0, 3, step, 0)

    class Reduce:
        def __init__(self, refs, target):
            (self.total, self.own_t, self.other_t, self.other_win, self.send_b, self.recv_b,
             self.send_c, self.recv_c, self.own, self.kept, self.pair_sem, self.send_b_sem, self.recv_b_sem,
             self.send_c_sem, self.recv_c_sem) = refs
            self.target = target
            self.part = self.own.shape[0]
            self.half = n_dp // 2
            self.source = dp // self.half
            self.local = self.source == core
            self.flip = depth // (n_depth // 2)

        def pair_copy(self, source, target, index):
            return pltpu.make_async_remote_copy(
                src_ref=source, dst_ref=target,
                send_sem=self.pair_sem.at[2 * index], recv_sem=self.pair_sem.at[2 * index + 1],
                device_id=core_id, device_id_type=MESH,
            )

        def win_copy(self, win):
            planes = pl.ds(1 - core, EDGE + 1)
            return self.pair_copy(win.at[planes], self.other_win.at[planes], 0)

        def win_wait(self, win):
            self.win_copy(win).wait()

        def grad_copy(self):
            return self.pair_copy(self.own_t, self.other_t, 1)

        def share_grad(self, values):
            self.own_t[...] = values.T
            self.grad_copy().start()

        def rows_at(self, block, z):
            start = (block * n_depth + z) * 2 * self.part + core * (channels // 2)
            return pl.ds(pl.multiple_of(start, 8), 2 * self.part)

        def b_copy(self, t, z, side):
            target = core * self.half + t
            slot = (dp - target - 1 + n_dp) % n_dp
            return pltpu.make_async_remote_copy(
                src_ref=self.send_b.at[t, z, side], dst_ref=self.recv_b.at[slot, z],
                send_sem=self.send_b_sem.at[t, z, side], recv_sem=self.recv_b_sem.at[slot, z],
                device_id=(target, depth * 2 + side), device_id_type=MESH,
            )

        def b_arrival(self, j, z):
            return pltpu.make_async_remote_copy(
                src_ref=self.send_b.at[0, z, 0], dst_ref=self.recv_b.at[j, z],
                send_sem=self.send_b_sem.at[0, z, 0], recv_sem=self.recv_b_sem.at[j, z],
                device_id=core_id, device_id_type=MESH,
            )

        def leaves(self, t, side):
            return jnp.logical_or(dp != core * self.half + t, core != side)

        def send_chunk(self, t, z):
            block = self.total[self.rows_at(t, z), :]
            for side in range(2):
                self.send_b[t, z, side] = block[side * self.part : (side + 1) * self.part].astype(BF16)

                @pl.when(self.leaves(t, side))
                def _():
                    self.b_copy(t, z, side).start()

        def mirrored(self, index, count):
            return index + self.flip * (count - 1 - 2 * index)

        def depths(self):
            near = jnp.minimum(depth, n_depth - 1 - depth)
            order = list(range(n_depth - 1, n_depth // 2 - 1, -1))
            if n_depth == 4:
                order += [1 - near, near]
            else:
                order += list(range(n_depth // 2 - 1, -1, -1))
            return [self.mirrored(z, n_depth) for z in order]

        def multiply(self, win):
            groups = (TAPS + 1) // 4
            order = [2, 3, 5, 6, 1, 4, 0]
            depths = self.depths()
            waiting = [(t, n_depth - 1 - k) for k in range(n_depth) for t in range(self.half)]
            if n_depth == 4:
                needs = {1: (0, 2), 0: (0, 2)}
            else:
                needs = {}
            done = set()
            size = 2 * channels
            for group in order:
                corners = []
                for flip in range(2):
                    at = groups - 1 - group if flip else group
                    for side in range(2):
                        taps = [2 * at + index + side * (TAPS // 2) for index in range(2)]
                        corners.append([(tap // 9, tap // 3 % 3, tap % 3) for tap in taps])
                columns = []
                for index in range(2):
                    at = []
                    for axis in range(3):
                        a, b, c, d = (corner[index][axis] for corner in corners)
                        low = a + core * (b - a)
                        high = c + core * (d - c)
                        at.append(pl.ds(low + self.flip * (high - low), EDGE))
                    columns.append(jnp.concatenate(
                        [
                            w[tuple(at)].reshape(EDGE * plane_rows, channels)
                            for w in (win, self.other_win)
                        ],
                        axis=0,
                    ))
                both = jnp.concatenate([self.own_t[...], self.other_t[...]], axis=1)
                product = jnp.dot(
                    both, jnp.concatenate(columns, axis=1), preferred_element_type=F32
                )
                product = jnp.concatenate(
                    [product[:, :channels].T, product[:, channels:].T], axis=0
                )
                start = pl.multiple_of(self.mirrored(group, groups) * size, size)
                self.total[pl.ds(start, size), :] = product
                done.add(group)
                for t, z in list(waiting):
                    low, high = needs.get(z, (z, z + 1))
                    begin = (t * n_depth + low) * 2 * self.part
                    end = (t * n_depth + high) * 2 * self.part + channels // 2
                    if all(g in done for g in range(begin // size, -(-end // size))):
                        waiting.remove((t, z))
                        self.send_chunk(self.mirrored(t, self.half), depths[n_depth - 1 - z])

        def c_copy(self, z):
            slot = (depth - z - 1 + n_depth) % n_depth
            return pltpu.make_async_remote_copy(
                src_ref=self.send_c.at[z], dst_ref=self.recv_c.at[slot],
                send_sem=self.send_c_sem.at[z], recv_sem=self.recv_c_sem.at[slot],
                device_id=(dp, z * 2 + core), device_id_type=MESH,
            )

        def c_arrival(self, slot):
            return pltpu.make_async_remote_copy(
                src_ref=self.send_c.at[0], dst_ref=self.recv_c.at[slot],
                send_sem=self.send_c_sem.at[0], recv_sem=self.recv_c_sem.at[slot],
                device_id=core_id, device_id_type=MESH,
            )

        def forward(self, low, high):
            for z in self.depths()[low:high]:
                @pl.when(self.local)
                def _():
                    block = self.total[self.rows_at(dp - self.source * self.half, z), :]
                    self.own[...] = jnp.where(core == 0, block[: self.part], block[self.part :])

                @pl.when(jnp.logical_not(self.local))
                def _():
                    self.b_arrival(n_dp - 1, z).wait_recv()
                    self.own[...] = self.recv_b[n_dp - 1, z].astype(F32)

                for j in range(n_dp - 1):
                    self.b_arrival(j, z).wait_recv()
                summed = self.own[...]
                for j in range(n_dp - 1):
                    summed = summed + self.recv_b[j, z].astype(F32)

                @pl.when(z != depth)
                def _():
                    self.send_c[z] = summed.astype(BF16)
                    self.c_copy(z).start()

                @pl.when(z == depth)
                def _():
                    self.kept[...] = summed

        def finish(self):
            summed = self.kept[...]
            for slot in range(n_depth - 1):
                self.c_arrival(slot).wait_recv()
                summed = summed + self.recv_c[slot].astype(F32)
            self.target[...] = summed * factor

        def drain(self):
            for t in range(self.half):
                for side in range(2):
                    @pl.when(self.leaves(t, side))
                    def _():
                        for z in range(n_depth):
                            self.b_copy(t, z, side).wait_send()

            for z in range(n_depth):
                @pl.when(z != depth)
                def _():
                    self.c_copy(z).wait_send()

    if fused:
        count = len(reduce_refs) // 2
        red2 = Reduce(reduce_refs[:count], g2_ref)
        red1 = Reduce(reduce_refs[count:], g1_ref)

    def flat_of(win):
        return win[1:5, 1:5, 1:5].reshape(EDGE * plane_rows, channels)

    def first_plane(plane, values):
        values = values * occ[plane].astype(F32)
        first[plane] = values
        win_b[plane + 1, 1:5, 1:5] = (values * jax.nn.sigmoid(values)).astype(BF16)

    fill(win_a, 0, 0)
    loads[3].wait()
    inside(win_a, w1_ref)
    summed_planes(first_plane, inner)
    wait_pair(*cell_copies())
    low_key = jnp.where(
        jnp.logical_and(beside_lane, has_low), cells_low[...] - layer_key, own_key
    )
    high_key = jnp.where(
        jnp.logical_and(beside_lane, has_high), cells_high[...] + layer_key, own_key
    )

    for d in directions:
        if d[0] != 0:
            pickers[d] = picker(low_key if d[0] < 0 else high_key, *d)
    wait_pair(*halo_copies(0))
    fill(win_a, 0, 1)
    across(win_a, w1_ref)
    summed_planes(first_plane, outer)
    send_halo(1, win_b)
    if fused:
        red1.win_copy(win_a).start()
    loads[5].wait()
    loads[4].wait()
    stage_cot[...] = cot_ref[...].astype(F32)
    for plane in range(EDGE):
        cot = jnp.stack([stage_cot[rows_of(plane, index), :] for index in range(EDGE * EDGE)])
        cot = cot.reshape(EDGE, EDGE, bricks, channels)
        cot_cube[plane] = (cot * occ[plane].astype(F32)).astype(BF16)
    fill(win_b, 1, 0)
    inside(win_b, w2_ref)

    def second_plane(plane, values):
        occupancy = occ[plane].astype(F32)
        total = win_a[plane + 1, 1:5, 1:5].astype(F32) + values * occupancy
        resid[plane] = total
        gradient = (cot_cube[plane].astype(F32) * silu_slope(total)).astype(BF16)
        win_c[plane + 1, 1:5, 1:5] = gradient

    summed_planes(second_plane, inner)
    for plane in range(EDGE):
        first[plane] = silu_slope(first[plane]) * occ[plane].astype(F32)
    wait_pair(*halo_copies(1))
    fill(win_b, 1, 1)
    if fused:
        red2.win_copy(win_b).start()
    across(win_b, w2_ref)
    summed_planes(second_plane, outer)
    send_halo(2, win_c)

    if fused:
        red2.share_grad(flat_of(win_c))
    else:
        weight_grad(win_b, flat_of(win_c), g2_ref)

    def third_plane(plane, values):
        gradient = (values * first[plane]).astype(BF16)
        win_d[plane + 1, 1:5, 1:5] = gradient

    fill(win_c, 2, 0)
    over_planes(third_plane, win_c, w2_ref, inner, True)
    if fused:
        red2.win_wait(win_b)
        red2.grad_copy().wait()
        red2.multiply(win_b)
    wait_pair(*halo_copies(2))
    fill(win_c, 2, 1)
    over_planes(third_plane, win_c, w2_ref, outer, True)
    send_halo(3, win_d)
    if fused:
        red1.share_grad(flat_of(win_d))
    else:
        weight_grad(win_a, flat_of(win_d), g1_ref)

    def fourth_plane(plane, values):
        values = win_c[plane + 1, 1:5, 1:5].astype(F32) + values
        scatter_plane(stage, plane, values * occ[plane].astype(F32))

    fill(win_d, 3, 0)
    over_planes(fourth_plane, win_d, w1_ref, inner, True)
    if fused:
        red1.win_wait(win_a)
        red1.grad_copy().wait()
        red2.forward(0, 1)
        red1.multiply(win_a)
        red2.forward(1, n_depth - 1)
    for plane in range(EDGE):
        total = resid[plane]
        scatter_plane(stage_cot, plane, total * jax.nn.sigmoid(total))
    out_ref[...] = stage_cot[...].astype(BF16)
    wait_pair(*halo_copies(3))
    fill(win_d, 3, 1)
    over_planes(fourth_plane, win_d, w1_ref, outer, True)
    if fused:
        red2.forward(n_depth - 1, n_depth)
    grad_in_ref[...] = stage[...].astype(BF16)
    if fused:
        red1.forward(0, n_depth - 1)
        red2.finish()
        red1.forward(n_depth - 1, n_depth)
        red1.finish()
        red2.drain()
        red1.drain()


def writer(*refs):
    count = len(refs) // 2
    sems = refs[-1]
    copies = [
        pltpu.make_async_copy(refs[index], refs[count + index], sems.at[index])
        for index in range(count)
    ]
    for copy in copies:
        copy.start()
    for copy in copies:
        copy.wait()


def shards(n_dp, n_space, features, weight_one, weight_two, cotangent, brick_cell, voxel_mask):
    bricks, channels = features.shape[1], features.shape[3]
    factor = 1.0 / math.sqrt(n_dp * n_space * bricks * 64)
    rows = TAPS * channels
    devices = n_dp * n_space
    fused = (
        n_space % 2 == 0 and n_dp % 2 == 0 and rows % devices == 0
        and (rows // devices * 2) % 8 == 0
    )
    cube = (EDGE, EDGE, EDGE, bricks, channels)
    flat = (bricks * EDGE**3, channels)
    window = (EDGE + 2, EDGE + 2, EDGE + 2, bricks, channels)
    plane = (EDGE, EDGE, bricks, channels)
    mask = voxel_mask[0]
    scratch = [
        pltpu.VMEM(flat, BF16), pltpu.VMEM(flat, BF16),
        pltpu.VMEM(mask.shape, jnp.int32), pltpu.VMEM(brick_cell.shape, jnp.int32),
        pltpu.VMEM(weight_one.shape, BF16), pltpu.VMEM(weight_two.shape, BF16),
        pltpu.SemaphoreType.DMA((6,)),
        pltpu.VMEM(window, BF16), pltpu.VMEM(window, BF16),
        pltpu.VMEM(window, BF16), pltpu.VMEM(window, BF16),
        pltpu.VMEM(cube, F32), pltpu.VMEM(cube, F32),
        pltpu.VMEM((EDGE, 8 * bricks, 2 * channels), F32),
        pltpu.VMEM(cube, BF16), pltpu.VMEM(cube, BF16),
        pltpu.VMEM(flat, F32), pltpu.VMEM(flat, F32),
        pltpu.VMEM((channels, flat[0]), BF16),
        pltpu.VMEM((4,) + plane, BF16), pltpu.VMEM((4,) + plane, BF16),
        pltpu.VMEM((4,) + plane, BF16), pltpu.VMEM((4,) + plane, BF16),
        pltpu.VMEM((8, 128), F32), pltpu.VMEM((8, 128), F32), pltpu.VMEM((8, 128), F32),
        pltpu.SemaphoreType.DMA((4, 2)), pltpu.SemaphoreType.DMA((4, 2)),
        pltpu.SemaphoreType.DMA((4,)),
    ]
    if fused:
        part = rows // devices
        n_depth = n_space // 2
        half = n_dp // 2
        for _ in range(2):
            scratch += [
                pltpu.VMEM(((TAPS + 1) // 2 * channels, channels), F32),
                pltpu.VMEM((channels, flat[0]), BF16), pltpu.VMEM((channels, flat[0]), BF16),
                pltpu.VMEM(window, BF16),
                pltpu.VMEM((half, n_depth, 2, part, channels), BF16),
                pltpu.VMEM((n_dp, n_depth, part, channels), BF16),
                pltpu.VMEM((n_depth, part, channels), BF16),
                pltpu.VMEM((n_depth - 1, part, channels), BF16),
                pltpu.VMEM((part, channels), F32),
                pltpu.VMEM((part, channels), F32),
                pltpu.SemaphoreType.DMA((4,)),
                pltpu.SemaphoreType.DMA((half, n_depth, 2)),
                pltpu.SemaphoreType.DMA((n_dp, n_depth)),
                pltpu.SemaphoreType.DMA((n_depth,)),
                pltpu.SemaphoreType.DMA((n_depth - 1,)),
            ]
        grad_shape = (part, channels)
    else:
        grad_shape = (rows, channels)
    vmem = pl.BlockSpec(memory_space=pltpu.VMEM)
    hbm = pl.BlockSpec(memory_space=pltpu.HBM)
    results = pl.pallas_call(
        functools.partial(kernel, n_dp, n_space, fused, factor),
        out_shape=(
            jax.ShapeDtypeStruct(flat, BF16), jax.ShapeDtypeStruct(flat, BF16),
            jax.ShapeDtypeStruct(grad_shape, F32), jax.ShapeDtypeStruct(grad_shape, F32),
        ),
        in_specs=[hbm] * 6,
        out_specs=(vmem,) * 4,
        scratch_shapes=scratch,
        compiler_params=pltpu.CompilerParams(
            collective_id=0, has_side_effects=True, vmem_limit_bytes=VMEM_LIMIT
        ),
    )(*(
        pltpu.with_memory_space_constraint(argument, pltpu.HBM)
        for argument in (
            features.reshape(flat), cotangent.reshape(flat), mask, brick_cell,
            weight_one, weight_two,
        )
    ))

    if fused:
        results = pl.pallas_call(
            writer,
            out_shape=tuple(jax.ShapeDtypeStruct(r.shape, r.dtype) for r in results),
            in_specs=[vmem] * 4,
            out_specs=(hbm,) * 4,
            scratch_shapes=[pltpu.SemaphoreType.DMA((4,))],
            compiler_params=pltpu.CompilerParams(vmem_limit_bytes=1024 * 1024),
        )(*results)
    block_out, input_grad, grad_one, grad_two = results
    grad_one, grad_two = grad_one.reshape(-1), grad_two.reshape(-1)
    if not fused:
        grad_one, grad_two = (
            lax.psum_scatter(g, ("dp", "space"), scatter_dimension=0, tiled=True) * factor
            for g in (grad_one, grad_two)
        )
    shape = features.shape
    return (block_out.reshape(shape), input_grad.reshape(shape), grad_one, grad_two)


def solution(mesh):
    return jax.shard_map(
        functools.partial(shards, mesh.shape["dp"], mesh.shape["space"]),
        mesh=mesh,
        in_specs=(
            P("dp", "space", None, None),
            P(),
            P(),
            P("dp", "space", None, None),
            P("dp", "space"),
            P("dp", "space", None),
        ),
        out_specs=(
            P("dp", "space", None, None),
            P("dp", "space", None, None),
            P(("dp", "space")),
            P(("dp", "space")),
        ),
        check_vma=False,
    )
```

```python
import functools
import math

import jax
import jax.numpy as jnp
from jax import lax
from jax.experimental import pallas as pl
from jax.experimental.pallas import tpu as pltpu
from jax.sharding import PartitionSpec as P

LAYERS_X = 2
SIDE = 8
EDGE = 4
TAPS = 27
FAR = -1000000.0
MESH = pl.DeviceIdType.MESH
F32 = jnp.float32
BF16 = jnp.bfloat16
VMEM_LIMIT = 48 * 1024 * 1024

SPANS = {-1: (0, 1, 3, 4), 0: (1, 5, 0, 4), 1: (5, 6, 0, 1)}


def silu_slope(values):
    logistic = jax.nn.sigmoid(values)
    return logistic * (1.0 + values * (1.0 - logistic))


def kernel(
    n_dp, n_space, fused, factor,
    feat_hbm, cot_hbm, mask_hbm, cell_hbm, w1_hbm, w2_hbm,
    out_ref, grad_in_ref, g1_ref, g2_ref,
    feat_ref, cot_ref, mask_ref, cell_ref, w1_ref, w2_ref, load_sem,
    win_a, win_b, win_c, win_d, first, resid, sums, occ, cot_cube, stage, stage_cot, g_t,
    send_low, send_high, from_low, from_high, cells, cells_low, cells_high,
    halo_send, halo_recv, cell_sem, *reduce_refs,
):
    bricks = mask_ref.shape[0]
    channels = feat_ref.shape[1]
    voxels = EDGE**3
    plane_rows = EDGE * EDGE * bricks
    dp = lax.axis_index("dp")
    space = lax.axis_index("space")
    has_low = space > 0
    has_high = space < n_space - 1
    low_id = (dp, lax.max(space - 1, 0))
    high_id = (dp, lax.min(space + 1, n_space - 1))
    core = space % 2
    depth = space // 2
    n_depth = n_space // 2

    core_id = (dp, depth * 2 + 1 - core)
    dp_ids = [((dp + j) % n_dp, space) for j in range(1, n_dp)]
    space_ids = [(dp, (space + j) % n_space) for j in range(1, n_space)]
    cross_ids = [((dp + j) % n_dp, core_id[1]) for j in range(1, n_dp)]

    loads = [
        pltpu.make_async_copy(source, target, load_sem.at[index])
        for index, (source, target) in enumerate([
            (cell_hbm, cell_ref), (mask_hbm, mask_ref), (feat_hbm, feat_ref),
            (w1_hbm, w1_ref), (cot_hbm, cot_ref), (w2_hbm, w2_ref),
        ])
    ]
    for load in loads:
        load.start()

    barrier = pltpu.get_barrier_semaphore()

    if fused:
        for partner in space_ids + dp_ids + cross_ids:
            pl.semaphore_signal(barrier, inc=1, device_id=partner, device_id_type=MESH)
        expected = n_space + 2 * n_dp - 3
    else:
        @pl.when(has_low)
        def _():
            pl.semaphore_signal(barrier, inc=1, device_id=low_id, device_id_type=MESH)

        @pl.when(has_high)
        def _():
            pl.semaphore_signal(barrier, inc=1, device_id=high_id, device_id_type=MESH)

        expected = has_low.astype(jnp.int32) + has_high.astype(jnp.int32)

    def halo_copies(phase):
        down = pltpu.make_async_remote_copy(
            src_ref=send_low.at[phase], dst_ref=from_high.at[phase],
            send_sem=halo_send.at[phase, 0], recv_sem=halo_recv.at[phase, 0],
            device_id=low_id, device_id_type=MESH,
        )
        up = pltpu.make_async_remote_copy(
            src_ref=send_high.at[phase], dst_ref=from_low.at[phase],
            send_sem=halo_send.at[phase, 1], recv_sem=halo_recv.at[phase, 1],
            device_id=high_id, device_id_type=MESH,
        )
        return down, up

    def cell_copies():
        down = pltpu.make_async_remote_copy(
            src_ref=cells, dst_ref=cells_high,
            send_sem=cell_sem.at[0], recv_sem=cell_sem.at[1],
            device_id=low_id, device_id_type=MESH,
        )
        up = pltpu.make_async_remote_copy(
            src_ref=cells, dst_ref=cells_low,
            send_sem=cell_sem.at[2], recv_sem=cell_sem.at[3],
            device_id=high_id, device_id_type=MESH,
        )
        return down, up

    def start_pair(down, up):
        @pl.when(has_low)
        def _():
            down.start()

        @pl.when(has_high)
        def _():
            up.start()

    def wait_pair(down, up):
        @pl.when(has_low)
        def _():
            down.wait_send()
            up.wait_recv()

        @pl.when(has_high)
        def _():
            up.wait_send()
            down.wait_recv()

    def send_halo(phase, win):
        send_low[phase] = win[1, 1:5, 1:5]
        send_high[phase] = win[4, 1:5, 1:5]
        start_pair(*halo_copies(phase))

    @pl.when(jnp.logical_not(has_low))
    def _():
        from_low[...] = jnp.zeros_like(from_low)
        cells_low[...] = jnp.zeros_like(cells_low)

    @pl.when(jnp.logical_not(has_high))
    def _():
        from_high[...] = jnp.zeros_like(from_high)
        cells_high[...] = jnp.zeros_like(cells_high)

    loads[0].wait()
    cell = cell_ref[...]
    key = (
        (cell // (SIDE * SIDE) + LAYERS_X) * 100 + (cell // SIDE % SIDE + 1) * 10 + cell % SIDE + 1
    ).astype(F32)
    square = (bricks, bricks)
    diagonal = lax.broadcasted_iota(jnp.int32, square, 0) == lax.broadcasted_iota(jnp.int32, square, 1)
    column = jnp.sum(
        jnp.where(diagonal, jnp.broadcast_to(key, square), 0.0), axis=1, keepdims=True
    )
    col_key = jnp.broadcast_to(column, (bricks, 128))
    brick = lax.broadcasted_iota(jnp.int32, (bricks, 128), 0)
    lane_of = lax.broadcasted_iota(jnp.int32, (bricks, 128), 1)
    own_row = jnp.sum(jnp.where(brick == lane_of, col_key, 0.0), axis=0, keepdims=True)
    beside_row = jnp.sum(jnp.where(brick + bricks == lane_of, col_key, 0.0), axis=0, keepdims=True)
    cells[...] = jnp.broadcast_to(beside_row, (8, 128))

    loads[1].wait()
    loads[2].wait()
    stage[...] = feat_ref[...].astype(F32)
    occupied = mask_ref[...].astype(F32)

    def place(planes):
        for x in planes:
            for y in range(EDGE):
                for z in range(EDGE):
                    voxel = (x * EDGE + y) * EDGE + z
                    kept = jnp.broadcast_to(occupied[:, voxel : voxel + 1], (bricks, channels))
                    occ[x, y, z] = kept.astype(BF16)
                    rows = stage[pl.ds(voxel, bricks, stride=voxels), :] * kept
                    win_a[x + 1, y + 1, z + 1] = rows.astype(BF16)

    outer, inner = (0, EDGE - 1), tuple(range(1, EDGE - 1))
    place(outer)
    pl.semaphore_wait(barrier, expected)
    start_pair(*cell_copies())
    send_halo(0, win_a)
    place(inner)

    lane = lax.broadcasted_iota(jnp.int32, (8, 128), 1)
    beside_lane = jnp.logical_and(lane >= bricks, lane < 2 * bricks)
    own_key = jnp.where(lane < bricks, jnp.broadcast_to(own_row, (8, 128)), FAR)
    layer_key = 100.0 * LAYERS_X
    def picker(row_key, shift_x, shift_y, shift_z):
        width = bricks if shift_x == 0 else 2 * bricks
        row_key = jnp.concatenate([row_key] * (bricks // 8), axis=0)
        wanted = col_key + float(shift_x * 100 + shift_y * 10 + shift_z)
        return jnp.where(wanted == row_key, 1.0, 0.0)[:, :width].astype(BF16)

    directions = [
        (x, y, z) for x in (0, -1, 1) for y in (-1, 0, 1) for z in (-1, 0, 1) if (x, y, z) != (0, 0, 0)
    ]
    pickers = {d: picker(own_key, *d) for d in directions if d[0] == 0}

    def fill(win, phase, which):
        for direction in directions:
            shift_x, shift_y, shift_z = direction
            if (shift_x == 0) != (which == 0):
                continue
            wx0, wx1, sx0, sx1 = SPANS[shift_x]
            wy0, wy1, sy0, sy1 = SPANS[shift_y]
            wz0, wz1, sz0, sz1 = SPANS[shift_z]
            source = win[sx0 + 1 : sx1 + 1, sy0 + 1 : sy1 + 1, sz0 + 1 : sz1 + 1]
            if shift_x != 0:
                halo = from_low if shift_x < 0 else from_high
                beside = halo[phase, sy0:sy1, sz0:sz1][None]
                source = jnp.concatenate([source, beside], axis=3)
            count = (sx1 - sx0) * (sy1 - sy0) * (sz1 - sz0)
            source = source.reshape(count, source.shape[3], channels)
            pick = pickers[direction]
            pick = jnp.broadcast_to(pick[None], (count,) + pick.shape)
            rows = lax.dot_general(
                pick, source, (((2,), (1,)), ((0,), (0,))), preferred_element_type=F32
            ).astype(BF16)
            win[wx0:wx1, wy0:wy1, wz0:wz1] = rows.reshape(
                wx1 - wx0, wy1 - wy0, wz1 - wz0, bricks, channels
            )

    def conv_rows(win, weight, planes, transposed, steps=(0, 1, 2)):
        lefts, rights = [], []
        empty = jnp.zeros((channels, channels), BF16)
        for dx in steps:
            for dy in range(3):
                for z in range(4):
                    rows = [
                        win[plane + dx, dy : dy + 4, z + 2 * half][:, None]
                        for plane in planes for half in range(2)
                    ]
                    rows = [
                        jnp.concatenate(rows[2 * p : 2 * p + 2], axis=1)[None]
                        for p in range(len(planes))
                    ]
                    rows = jnp.concatenate(rows, axis=0)
                    lefts.append(rows.reshape(len(planes) * 8 * bricks, channels))
                tap = 9 * dx + 3 * dy
                if transposed:
                    one, two, three = (weight[TAPS - 1 - tap - dz] for dz in range(3))
                else:
                    one, two, three = (weight[tap + dz] for dz in range(3))
                for pair in ((one, empty), (two, one), (three, two), (empty, three)):
                    rights.append(jnp.concatenate(pair, axis=0 if transposed else 1))
        left = jnp.concatenate(lefts, axis=1)
        right = jnp.concatenate(rights, axis=1 if transposed else 0)
        summed = lax.dot_general(
            left, right, (((1,), (1 if transposed else 0,)), ((), ())), preferred_element_type=F32
        )
        return summed.reshape(len(planes), 8 * bricks, 2 * channels)

    def as_plane(summed):
        summed = summed.reshape(EDGE, 2, bricks, 2 * channels)
        summed = jnp.stack([summed[..., :channels], summed[..., channels:]], axis=2)
        return summed.reshape(EDGE, EDGE, bricks, channels)

    def over_planes(body, win, weight, planes, transposed=False):
        values = conv_rows(win, weight, planes, transposed)
        for index, plane in enumerate(planes):
            body(plane, as_plane(values[index]))

    def inside(win, weight, transposed=False, steps=(1, 2, 0)):
        for dx in steps:
            if dx == 1:
                sums[...] = conv_rows(win, weight, range(EDGE), transposed, (1,))
            elif dx == 2:
                sums[: EDGE - 1] += conv_rows(win, weight, range(EDGE - 1), transposed, (2,))
            else:
                sums[1:] += conv_rows(win, weight, range(1, EDGE), transposed, (0,))

    def across(win, weight, transposed=False):
        sums[:1] += conv_rows(win, weight, (0,), transposed, (0,))
        sums[EDGE - 1 :] += conv_rows(win, weight, (EDGE - 1,), transposed, (2,))

    def summed_planes(body, planes):
        for plane in planes:
            body(plane, as_plane(sums[plane]))

    def rows_of(plane, index):
        return pl.ds(plane * EDGE * EDGE + index, bricks, stride=voxels)

    def scatter_plane(target, plane, values):
        for index in range(EDGE * EDGE):
            target[rows_of(plane, index), :] = values[index // EDGE, index % EDGE]

    def weight_grad(win, values, target):
        g_t[...] = values.T

        def step(dx, carry):
            pieces = [
                win[pl.ds(dx, 4), dy : dy + 4, dz : dz + 4].reshape(EDGE * plane_rows, channels)
                for dy in range(3) for dz in range(3)
            ]
            product = jnp.dot(
                g_t[...], jnp.concatenate(pieces, axis=1), preferred_element_type=F32
            )
            for tap in range(9):
                start = pl.multiple_of((dx * 9 + tap) * channels, channels)
                target[pl.ds(start, channels), :] = product[:, tap * channels : (tap + 1) * channels].T
            return carry

        lax.fori_loop(0, 3, step, 0)

    class Reduce:
        def __init__(self, refs, target):
            (self.total, self.own_t, self.other_t, self.other_win, self.send_b, self.recv_b,
             self.send_c, self.recv_c, self.own, self.kept, self.pair_sem, self.send_b_sem, self.recv_b_sem,
             self.send_c_sem, self.recv_c_sem) = refs
            self.target = target
            self.part = self.own.shape[0]
            self.half = n_dp // 2
            self.source = dp // self.half
            self.local = self.source == core
            self.flip = depth // (n_depth // 2)

        def pair_copy(self, source, target, index):
            return pltpu.make_async_remote_copy(
                src_ref=source, dst_ref=target,
                send_sem=self.pair_sem.at[2 * index], recv_sem=self.pair_sem.at[2 * index + 1],
                device_id=core_id, device_id_type=MESH,
            )

        def win_copy(self, win, edge):
            planes = pl.ds((1 - core) * (EDGE + 1), 1) if edge else pl.ds(1, EDGE)
            return self.pair_copy(win.at[planes], self.other_win.at[planes], 3 if edge else 0)

        def win_wait(self, win):
            for edge in range(2):
                self.win_copy(win, edge).wait()

        def grad_copy(self, half):
            rows = EDGE * plane_rows // 2
            columns = pl.ds(half * rows, rows)
            return self.pair_copy(self.own_t.at[:, columns], self.other_t.at[:, columns], 1 + half)

        def share_grad(self, win, half):
            rows = EDGE * plane_rows // 2
            planes = outer if half else inner
            values = jnp.concatenate(
                [win[plane + 1, 1:5, 1:5].reshape(plane_rows, channels) for plane in planes], axis=0
            )
            self.own_t[:, half * rows : (half + 1) * rows] = values.T
            self.grad_copy(half).start()

        def grad_wait(self):
            for half in range(2):
                self.grad_copy(half).wait()

        def rows_at(self, block, z):
            start = (block * n_depth + z) * 2 * self.part + core * (channels // 2)
            return pl.ds(pl.multiple_of(start, 8), 2 * self.part)

        def b_copy(self, t, z, side):
            target = core * self.half + t
            slot = (dp - target - 1 + n_dp) % n_dp
            return pltpu.make_async_remote_copy(
                src_ref=self.send_b.at[t, z, side], dst_ref=self.recv_b.at[slot, z],
                send_sem=self.send_b_sem.at[t, z, side], recv_sem=self.recv_b_sem.at[slot, z],
                device_id=(target, depth * 2 + side), device_id_type=MESH,
            )

        def b_arrival(self, j, z):
            return pltpu.make_async_remote_copy(
                src_ref=self.send_b.at[0, z, 0], dst_ref=self.recv_b.at[j, z],
                send_sem=self.send_b_sem.at[0, z, 0], recv_sem=self.recv_b_sem.at[j, z],
                device_id=core_id, device_id_type=MESH,
            )

        def leaves(self, t, side):
            return jnp.logical_or(dp != core * self.half + t, core != side)

        def send_chunk(self, t, z):
            block = self.total[self.rows_at(t, z), :]
            for side in range(2):
                self.send_b[t, z, side] = block[side * self.part : (side + 1) * self.part].astype(BF16)

                @pl.when(self.leaves(t, side))
                def _():
                    self.b_copy(t, z, side).start()

        def mirrored(self, index, count):
            return index + self.flip * (count - 1 - 2 * index)

        def depths(self):
            near = jnp.minimum(depth, n_depth - 1 - depth)
            order = list(range(n_depth - 1, n_depth // 2 - 1, -1))
            if n_depth == 4:
                order += [1 - near, near]
            else:
                order += list(range(n_depth // 2 - 1, -1, -1))
            return [self.mirrored(z, n_depth) for z in order]

        def multiply(self, win):
            groups = (TAPS + 1) // 4
            order = [2, 3, 5, 6, 1, 4, 0]
            depths = self.depths()
            waiting = [(t, n_depth - 1 - k) for k in range(n_depth) for t in range(self.half)]
            if n_depth == 4:
                needs = {1: (0, 2), 0: (0, 2)}
            else:
                needs = {}
            done = set()
            size = 2 * channels
            for group in order:
                corners = []
                for flip in range(2):
                    at = groups - 1 - group if flip else group
                    for side in range(2):
                        taps = [2 * at + index + side * (TAPS // 2) for index in range(2)]
                        corners.append([(tap // 9, tap // 3 % 3, tap % 3) for tap in taps])
                columns = []
                for index in range(2):
                    at = []
                    for axis in range(3):
                        a, b, c, d = (corner[index][axis] for corner in corners)
                        low = a + core * (b - a)
                        high = c + core * (d - c)
                        at.append(low + self.flip * (high - low))
                    spans = [pl.ds(at[0] + 1, 2), pl.ds(at[0], 1), pl.ds(at[0] + EDGE - 1, 1)]
                    columns.append(jnp.concatenate(
                        [
                            w[span, pl.ds(at[1], EDGE), pl.ds(at[2], EDGE)].reshape(-1, channels)
                            for w in (win, self.other_win) for span in spans
                        ],
                        axis=0,
                    ))
                both = jnp.concatenate([self.own_t[...], self.other_t[...]], axis=1)
                product = jnp.dot(
                    both, jnp.concatenate(columns, axis=1), preferred_element_type=F32
                )
                product = jnp.concatenate(
                    [product[:, :channels].T, product[:, channels:].T], axis=0
                )
                start = pl.multiple_of(self.mirrored(group, groups) * size, size)
                self.total[pl.ds(start, size), :] = product
                done.add(group)
                for t, z in list(waiting):
                    low, high = needs.get(z, (z, z + 1))
                    begin = (t * n_depth + low) * 2 * self.part
                    end = (t * n_depth + high) * 2 * self.part + channels // 2
                    if all(g in done for g in range(begin // size, -(-end // size))):
                        waiting.remove((t, z))
                        self.send_chunk(self.mirrored(t, self.half), depths[n_depth - 1 - z])

        def c_copy(self, z):
            slot = (depth - z - 1 + n_depth) % n_depth
            return pltpu.make_async_remote_copy(
                src_ref=self.send_c.at[z], dst_ref=self.recv_c.at[slot],
                send_sem=self.send_c_sem.at[z], recv_sem=self.recv_c_sem.at[slot],
                device_id=(dp, z * 2 + core), device_id_type=MESH,
            )

        def c_arrival(self, slot):
            return pltpu.make_async_remote_copy(
                src_ref=self.send_c.at[0], dst_ref=self.recv_c.at[slot],
                send_sem=self.send_c_sem.at[0], recv_sem=self.recv_c_sem.at[slot],
                device_id=core_id, device_id_type=MESH,
            )

        def forward(self, low, high):
            for z in self.depths()[low:high]:
                @pl.when(self.local)
                def _():
                    block = self.total[self.rows_at(dp - self.source * self.half, z), :]
                    self.own[...] = jnp.where(core == 0, block[: self.part], block[self.part :])

                @pl.when(jnp.logical_not(self.local))
                def _():
                    self.b_arrival(n_dp - 1, z).wait_recv()
                    self.own[...] = self.recv_b[n_dp - 1, z].astype(F32)

                for j in range(n_dp - 1):
                    self.b_arrival(j, z).wait_recv()
                summed = self.own[...]
                for j in range(n_dp - 1):
                    summed = summed + self.recv_b[j, z].astype(F32)

                @pl.when(z != depth)
                def _():
                    self.send_c[z] = summed.astype(BF16)
                    self.c_copy(z).start()

                @pl.when(z == depth)
                def _():
                    self.kept[...] = summed

        def finish(self):
            summed = self.kept[...]
            for slot in range(n_depth - 1):
                self.c_arrival(slot).wait_recv()
                summed = summed + self.recv_c[slot].astype(F32)
            self.target[...] = summed * factor

        def drain(self):
            for t in range(self.half):
                for side in range(2):
                    @pl.when(self.leaves(t, side))
                    def _():
                        for z in range(n_depth):
                            self.b_copy(t, z, side).wait_send()

            for z in range(n_depth):
                @pl.when(z != depth)
                def _():
                    self.c_copy(z).wait_send()

    if fused:
        count = len(reduce_refs) // 2
        red2 = Reduce(reduce_refs[:count], g2_ref)
        red1 = Reduce(reduce_refs[count:], g1_ref)

    def flat_of(win):
        return win[1:5, 1:5, 1:5].reshape(EDGE * plane_rows, channels)

    def first_plane(plane, values):
        values = values * occ[plane].astype(F32)
        first[plane] = values
        win_b[plane + 1, 1:5, 1:5] = (values * jax.nn.sigmoid(values)).astype(BF16)

    fill(win_a, 0, 0)
    loads[3].wait()
    inside(win_a, w1_ref)
    summed_planes(first_plane, inner)
    wait_pair(*cell_copies())
    low_key = jnp.where(
        jnp.logical_and(beside_lane, has_low), cells_low[...] - layer_key, own_key
    )
    high_key = jnp.where(
        jnp.logical_and(beside_lane, has_high), cells_high[...] + layer_key, own_key
    )

    for d in directions:
        if d[0] != 0:
            pickers[d] = picker(low_key if d[0] < 0 else high_key, *d)
    wait_pair(*halo_copies(0))
    fill(win_a, 0, 1)
    across(win_a, w1_ref)
    summed_planes(first_plane, outer)
    send_halo(1, win_b)
    if fused:
        red1.win_copy(win_a, 0).start()
        red1.win_copy(win_a, 1).start()
    loads[5].wait()
    loads[4].wait()
    stage_cot[...] = cot_ref[...].astype(F32)
    for plane in range(EDGE):
        cot = jnp.stack([stage_cot[rows_of(plane, index), :] for index in range(EDGE * EDGE)])
        cot = cot.reshape(EDGE, EDGE, bricks, channels)
        cot_cube[plane] = (cot * occ[plane].astype(F32)).astype(BF16)
    fill(win_b, 1, 0)
    if fused:
        red2.win_copy(win_b, 0).start()
    inside(win_b, w2_ref)

    def second_plane(plane, values):
        occupancy = occ[plane].astype(F32)
        total = win_a[plane + 1, 1:5, 1:5].astype(F32) + values * occupancy
        resid[plane] = total
        gradient = (cot_cube[plane].astype(F32) * silu_slope(total)).astype(BF16)
        win_c[plane + 1, 1:5, 1:5] = gradient

    summed_planes(second_plane, inner)
    if fused:
        red2.share_grad(win_c, 0)
    for plane in range(EDGE):
        first[plane] = silu_slope(first[plane]) * occ[plane].astype(F32)
    wait_pair(*halo_copies(1))
    fill(win_b, 1, 1)
    if fused:
        red2.win_copy(win_b, 1).start()
    across(win_b, w2_ref)
    summed_planes(second_plane, outer)
    send_halo(2, win_c)

    if fused:
        red2.share_grad(win_c, 1)
    else:
        weight_grad(win_b, flat_of(win_c), g2_ref)

    def third_plane(plane, values):
        gradient = (values * first[plane]).astype(BF16)
        win_d[plane + 1, 1:5, 1:5] = gradient

    fill(win_c, 2, 0)
    inside(win_c, w2_ref, True, (1, 2))
    if fused:
        red2.win_wait(win_b)
        red2.grad_wait()
        red2.multiply(win_b)
    inside(win_c, w2_ref, True, (0,))
    summed_planes(third_plane, inner)
    if fused:
        red1.share_grad(win_d, 0)
    wait_pair(*halo_copies(2))
    fill(win_c, 2, 1)
    across(win_c, w2_ref, True)
    summed_planes(third_plane, outer)
    send_halo(3, win_d)
    if fused:
        red1.share_grad(win_d, 1)
    else:
        weight_grad(win_a, flat_of(win_d), g1_ref)

    def fourth_plane(plane, values):
        values = win_c[plane + 1, 1:5, 1:5].astype(F32) + values
        scatter_plane(stage, plane, values * occ[plane].astype(F32))

    fill(win_d, 3, 0)
    over_planes(fourth_plane, win_d, w1_ref, inner, True)
    if fused:
        red1.win_wait(win_a)
        red1.grad_wait()
        red1.multiply(win_a)
        red2.forward(0, 2)
    for plane in range(EDGE):
        total = resid[plane]
        scatter_plane(stage_cot, plane, total * jax.nn.sigmoid(total))
    out_ref[...] = stage_cot[...].astype(BF16)
    if fused:
        red2.forward(2, n_depth - 1)
    wait_pair(*halo_copies(3))
    fill(win_d, 3, 1)
    over_planes(fourth_plane, win_d, w1_ref, outer, True)
    if fused:
        red2.forward(n_depth - 1, n_depth)
    grad_in_ref[...] = stage[...].astype(BF16)
    if fused:
        red1.forward(0, n_depth - 1)
        red2.finish()
        red1.forward(n_depth - 1, n_depth)
        red1.finish()
        red2.drain()
        red1.drain()


def writer(*refs):
    count = len(refs) // 2
    sems = refs[-1]
    copies = [
        pltpu.make_async_copy(refs[index], refs[count + index], sems.at[index])
        for index in range(count)
    ]
    for copy in copies:
        copy.start()
    for copy in copies:
        copy.wait()


def shards(n_dp, n_space, features, weight_one, weight_two, cotangent, brick_cell, voxel_mask):
    bricks, channels = features.shape[1], features.shape[3]
    factor = 1.0 / math.sqrt(n_dp * n_space * bricks * 64)
    rows = TAPS * channels
    devices = n_dp * n_space
    fused = (
        n_space % 2 == 0 and n_dp % 2 == 0 and rows % devices == 0
        and (rows // devices * 2) % 8 == 0
    )
    cube = (EDGE, EDGE, EDGE, bricks, channels)
    flat = (bricks * EDGE**3, channels)
    window = (EDGE + 2, EDGE + 2, EDGE + 2, bricks, channels)
    plane = (EDGE, EDGE, bricks, channels)
    mask = voxel_mask[0]
    scratch = [
        pltpu.VMEM(flat, BF16), pltpu.VMEM(flat, BF16),
        pltpu.VMEM(mask.shape, jnp.int32), pltpu.VMEM(brick_cell.shape, jnp.int32),
        pltpu.VMEM(weight_one.shape, BF16), pltpu.VMEM(weight_two.shape, BF16),
        pltpu.SemaphoreType.DMA((6,)),
        pltpu.VMEM(window, BF16), pltpu.VMEM(window, BF16),
        pltpu.VMEM(window, BF16), pltpu.VMEM(window, BF16),
        pltpu.VMEM(cube, F32), pltpu.VMEM(cube, F32),
        pltpu.VMEM((EDGE, 8 * bricks, 2 * channels), F32),
        pltpu.VMEM(cube, BF16), pltpu.VMEM(cube, BF16),
        pltpu.VMEM(flat, F32), pltpu.VMEM(flat, F32),
        pltpu.VMEM((channels, flat[0]), BF16),
        pltpu.VMEM((4,) + plane, BF16), pltpu.VMEM((4,) + plane, BF16),
        pltpu.VMEM((4,) + plane, BF16), pltpu.VMEM((4,) + plane, BF16),
        pltpu.VMEM((8, 128), F32), pltpu.VMEM((8, 128), F32), pltpu.VMEM((8, 128), F32),
        pltpu.SemaphoreType.DMA((4, 2)), pltpu.SemaphoreType.DMA((4, 2)),
        pltpu.SemaphoreType.DMA((4,)),
    ]
    if fused:
        part = rows // devices
        n_depth = n_space // 2
        half = n_dp // 2
        for _ in range(2):
            scratch += [
                pltpu.VMEM(((TAPS + 1) // 2 * channels, channels), F32),
                pltpu.VMEM((channels, flat[0]), BF16), pltpu.VMEM((channels, flat[0]), BF16),
                pltpu.VMEM(window, BF16),
                pltpu.VMEM((half, n_depth, 2, part, channels), BF16),
                pltpu.VMEM((n_dp, n_depth, part, channels), BF16),
                pltpu.VMEM((n_depth, part, channels), BF16),
                pltpu.VMEM((n_depth - 1, part, channels), BF16),
                pltpu.VMEM((part, channels), F32),
                pltpu.VMEM((part, channels), F32),
                pltpu.SemaphoreType.DMA((8,)),
                pltpu.SemaphoreType.DMA((half, n_depth, 2)),
                pltpu.SemaphoreType.DMA((n_dp, n_depth)),
                pltpu.SemaphoreType.DMA((n_depth,)),
                pltpu.SemaphoreType.DMA((n_depth - 1,)),
            ]
        grad_shape = (part, channels)
    else:
        grad_shape = (rows, channels)
    vmem = pl.BlockSpec(memory_space=pltpu.VMEM)
    hbm = pl.BlockSpec(memory_space=pltpu.HBM)
    results = pl.pallas_call(
        functools.partial(kernel, n_dp, n_space, fused, factor),
        out_shape=(
            jax.ShapeDtypeStruct(flat, BF16), jax.ShapeDtypeStruct(flat, BF16),
            jax.ShapeDtypeStruct(grad_shape, F32), jax.ShapeDtypeStruct(grad_shape, F32),
        ),
        in_specs=[hbm] * 6,
        out_specs=(vmem,) * 4,
        scratch_shapes=scratch,
        compiler_params=pltpu.CompilerParams(
            collective_id=0, has_side_effects=True, vmem_limit_bytes=VMEM_LIMIT
        ),
    )(*(
        pltpu.with_memory_space_constraint(argument, pltpu.HBM)
        for argument in (
            features.reshape(flat), cotangent.reshape(flat), mask, brick_cell,
            weight_one, weight_two,
        )
    ))

    if fused:
        results = pl.pallas_call(
            writer,
            out_shape=tuple(jax.ShapeDtypeStruct(r.shape, r.dtype) for r in results),
            in_specs=[vmem] * 4,
            out_specs=(hbm,) * 4,
            scratch_shapes=[pltpu.SemaphoreType.DMA((4,))],
            compiler_params=pltpu.CompilerParams(vmem_limit_bytes=1024 * 1024),
        )(*results)
    block_out, input_grad, grad_one, grad_two = results
    grad_one, grad_two = grad_one.reshape(-1), grad_two.reshape(-1)
    if not fused:
        grad_one, grad_two = (
            lax.psum_scatter(g, ("dp", "space"), scatter_dimension=0, tiled=True) * factor
            for g in (grad_one, grad_two)
        )
    shape = features.shape
    return (block_out.reshape(shape), input_grad.reshape(shape), grad_one, grad_two)


def solution(mesh):
    return jax.shard_map(
        functools.partial(shards, mesh.shape["dp"], mesh.shape["space"]),
        mesh=mesh,
        in_specs=(
            P("dp", "space", None, None),
            P(),
            P(),
            P("dp", "space", None, None),
            P("dp", "space"),
            P("dp", "space", None),
        ),
        out_specs=(
            P("dp", "space", None, None),
            P("dp", "space", None, None),
            P(("dp", "space")),
            P(("dp", "space")),
        ),
        check_vma=False,
    )
```

```python
import functools
import math

import jax
import jax.numpy as jnp
from jax import lax
from jax.experimental import pallas as pl
from jax.experimental.pallas import tpu as pltpu
from jax.sharding import PartitionSpec as P

LAYERS_X = 2
SIDE = 8
EDGE = 4
TAPS = 27
FAR = -1000000.0
MESH = pl.DeviceIdType.MESH
F32 = jnp.float32
BF16 = jnp.bfloat16
VMEM_LIMIT = 48 * 1024 * 1024

SPANS = {-1: (0, 1, 3, 4), 0: (1, 5, 0, 4), 1: (5, 6, 0, 1)}


def silu_slope(values):
    logistic = jax.nn.sigmoid(values)
    return logistic * (1.0 + values * (1.0 - logistic))


def kernel(
    n_dp, n_space, fused, factor,
    feat_hbm, cot_hbm, mask_hbm, cell_hbm, w1_hbm, w2_hbm,
    out_ref, grad_in_ref, g1_ref, g2_ref,
    feat_ref, cot_ref, mask_ref, cell_ref, w1_ref, w2_ref, load_sem,
    win_a, win_b, win_c, win_d, first, resid, sums, occ, cot_cube, stage, stage_cot, g_t,
    send_low, send_high, from_low, from_high, cells, cells_low, cells_high,
    halo_send, halo_recv, cell_sem, *reduce_refs,
):
    bricks = mask_ref.shape[0]
    channels = feat_ref.shape[1]
    voxels = EDGE**3
    plane_rows = EDGE * EDGE * bricks
    dp = lax.axis_index("dp")
    space = lax.axis_index("space")
    has_low = space > 0
    has_high = space < n_space - 1
    low_id = (dp, lax.max(space - 1, 0))
    high_id = (dp, lax.min(space + 1, n_space - 1))
    core = space % 2
    depth = space // 2
    n_depth = n_space // 2

    core_id = (dp, depth * 2 + 1 - core)
    dp_ids = [((dp + j) % n_dp, space) for j in range(1, n_dp)]
    space_ids = [(dp, (space + j) % n_space) for j in range(1, n_space)]
    cross_ids = [((dp + j) % n_dp, core_id[1]) for j in range(1, n_dp)]

    loads = [
        pltpu.make_async_copy(source, target, load_sem.at[index])
        for index, (source, target) in enumerate([
            (cell_hbm, cell_ref), (mask_hbm, mask_ref), (feat_hbm, feat_ref),
            (w1_hbm, w1_ref), (cot_hbm, cot_ref), (w2_hbm, w2_ref),
        ])
    ]
    for load in loads:
        load.start()

    barrier = pltpu.get_barrier_semaphore()

    if fused:
        for partner in space_ids + dp_ids + cross_ids:
            pl.semaphore_signal(barrier, inc=1, device_id=partner, device_id_type=MESH)
        expected = n_space + 2 * n_dp - 3
    else:
        @pl.when(has_low)
        def _():
            pl.semaphore_signal(barrier, inc=1, device_id=low_id, device_id_type=MESH)

        @pl.when(has_high)
        def _():
            pl.semaphore_signal(barrier, inc=1, device_id=high_id, device_id_type=MESH)

        expected = has_low.astype(jnp.int32) + has_high.astype(jnp.int32)

    def halo_copies(phase):
        down = pltpu.make_async_remote_copy(
            src_ref=send_low.at[phase], dst_ref=from_high.at[phase],
            send_sem=halo_send.at[phase, 0], recv_sem=halo_recv.at[phase, 0],
            device_id=low_id, device_id_type=MESH,
        )
        up = pltpu.make_async_remote_copy(
            src_ref=send_high.at[phase], dst_ref=from_low.at[phase],
            send_sem=halo_send.at[phase, 1], recv_sem=halo_recv.at[phase, 1],
            device_id=high_id, device_id_type=MESH,
        )
        return down, up

    def cell_copies():
        down = pltpu.make_async_remote_copy(
            src_ref=cells, dst_ref=cells_high,
            send_sem=cell_sem.at[0], recv_sem=cell_sem.at[1],
            device_id=low_id, device_id_type=MESH,
        )
        up = pltpu.make_async_remote_copy(
            src_ref=cells, dst_ref=cells_low,
            send_sem=cell_sem.at[2], recv_sem=cell_sem.at[3],
            device_id=high_id, device_id_type=MESH,
        )
        return down, up

    def start_pair(down, up):
        @pl.when(has_low)
        def _():
            down.start()

        @pl.when(has_high)
        def _():
            up.start()

    def wait_pair(down, up):
        @pl.when(has_low)
        def _():
            down.wait_send()
            up.wait_recv()

        @pl.when(has_high)
        def _():
            up.wait_send()
            down.wait_recv()

    def send_halo(phase, win):
        send_low[phase] = win[1, 1:5, 1:5]
        send_high[phase] = win[4, 1:5, 1:5]
        start_pair(*halo_copies(phase))

    @pl.when(jnp.logical_not(has_low))
    def _():
        from_low[...] = jnp.zeros_like(from_low)
        cells_low[...] = jnp.zeros_like(cells_low)

    @pl.when(jnp.logical_not(has_high))
    def _():
        from_high[...] = jnp.zeros_like(from_high)
        cells_high[...] = jnp.zeros_like(cells_high)

    loads[0].wait()
    cell = cell_ref[...]
    key = (
        (cell // (SIDE * SIDE) + LAYERS_X) * 100 + (cell // SIDE % SIDE + 1) * 10 + cell % SIDE + 1
    ).astype(F32)
    square = (bricks, bricks)
    diagonal = lax.broadcasted_iota(jnp.int32, square, 0) == lax.broadcasted_iota(jnp.int32, square, 1)
    column = jnp.sum(
        jnp.where(diagonal, jnp.broadcast_to(key, square), 0.0), axis=1, keepdims=True
    )
    col_key = jnp.broadcast_to(column, (bricks, 128))
    brick = lax.broadcasted_iota(jnp.int32, (bricks, 128), 0)
    lane_of = lax.broadcasted_iota(jnp.int32, (bricks, 128), 1)
    own_row = jnp.sum(jnp.where(brick == lane_of, col_key, 0.0), axis=0, keepdims=True)
    beside_row = jnp.sum(jnp.where(brick + bricks == lane_of, col_key, 0.0), axis=0, keepdims=True)
    cells[...] = jnp.broadcast_to(beside_row, (8, 128))

    loads[1].wait()
    loads[2].wait()
    stage[...] = feat_ref[...].astype(F32)
    occupied = mask_ref[...].astype(F32)

    def place(planes):
        for x in planes:
            for y in range(EDGE):
                for z in range(EDGE):
                    voxel = (x * EDGE + y) * EDGE + z
                    kept = jnp.broadcast_to(occupied[:, voxel : voxel + 1], (bricks, channels))
                    occ[x, y, z] = kept.astype(BF16)
                    rows = stage[pl.ds(voxel, bricks, stride=voxels), :] * kept
                    win_a[x + 1, y + 1, z + 1] = rows.astype(BF16)

    outer, inner = (0, EDGE - 1), tuple(range(1, EDGE - 1))
    place(outer)
    pl.semaphore_wait(barrier, expected)
    start_pair(*cell_copies())
    send_halo(0, win_a)
    place(inner)

    lane = lax.broadcasted_iota(jnp.int32, (8, 128), 1)
    beside_lane = jnp.logical_and(lane >= bricks, lane < 2 * bricks)
    own_key = jnp.where(lane < bricks, jnp.broadcast_to(own_row, (8, 128)), FAR)
    layer_key = 100.0 * LAYERS_X
    def picker(row_key, shift_x, shift_y, shift_z):
        width = bricks if shift_x == 0 else 2 * bricks
        row_key = jnp.concatenate([row_key] * (bricks // 8), axis=0)
        wanted = col_key + float(shift_x * 100 + shift_y * 10 + shift_z)
        return jnp.where(wanted == row_key, 1.0, 0.0)[:, :width].astype(BF16)

    directions = [
        (x, y, z) for x in (0, -1, 1) for y in (-1, 0, 1) for z in (-1, 0, 1) if (x, y, z) != (0, 0, 0)
    ]
    pickers = {d: picker(own_key, *d) for d in directions if d[0] == 0}

    def fill(win, phase, which):
        for direction in directions:
            shift_x, shift_y, shift_z = direction
            if (shift_x == 0) != (which == 0):
                continue
            wx0, wx1, sx0, sx1 = SPANS[shift_x]
            wy0, wy1, sy0, sy1 = SPANS[shift_y]
            wz0, wz1, sz0, sz1 = SPANS[shift_z]
            source = win[sx0 + 1 : sx1 + 1, sy0 + 1 : sy1 + 1, sz0 + 1 : sz1 + 1]
            if shift_x != 0:
                halo = from_low if shift_x < 0 else from_high
                beside = halo[phase, sy0:sy1, sz0:sz1][None]
                source = jnp.concatenate([source, beside], axis=3)
            count = (sx1 - sx0) * (sy1 - sy0) * (sz1 - sz0)
            source = source.reshape(count, source.shape[3], channels)
            pick = pickers[direction]
            pick = jnp.broadcast_to(pick[None], (count,) + pick.shape)
            rows = lax.dot_general(
                pick, source, (((2,), (1,)), ((0,), (0,))), preferred_element_type=F32
            ).astype(BF16)
            win[wx0:wx1, wy0:wy1, wz0:wz1] = rows.reshape(
                wx1 - wx0, wy1 - wy0, wz1 - wz0, bricks, channels
            )

    def conv_rows(win, weight, planes, transposed, steps=(0, 1, 2)):
        lefts, rights = [], []
        empty = jnp.zeros((channels, channels), BF16)
        for dx in steps:
            for dy in range(3):
                for z in range(4):
                    rows = [
                        win[plane + dx, dy : dy + 4, z + 2 * half][:, None]
                        for plane in planes for half in range(2)
                    ]
                    rows = [
                        jnp.concatenate(rows[2 * p : 2 * p + 2], axis=1)[None]
                        for p in range(len(planes))
                    ]
                    rows = jnp.concatenate(rows, axis=0)
                    lefts.append(rows.reshape(len(planes) * 8 * bricks, channels))
                tap = 9 * dx + 3 * dy
                if transposed:
                    one, two, three = (weight[TAPS - 1 - tap - dz] for dz in range(3))
                else:
                    one, two, three = (weight[tap + dz] for dz in range(3))
                for pair in ((one, empty), (two, one), (three, two), (empty, three)):
                    rights.append(jnp.concatenate(pair, axis=0 if transposed else 1))
        left = jnp.concatenate(lefts, axis=1)
        right = jnp.concatenate(rights, axis=1 if transposed else 0)
        summed = lax.dot_general(
            left, right, (((1,), (1 if transposed else 0,)), ((), ())), preferred_element_type=F32
        )
        return summed.reshape(len(planes), 8 * bricks, 2 * channels)

    def as_plane(summed):
        summed = summed.reshape(EDGE, 2, bricks, 2 * channels)
        summed = jnp.stack([summed[..., :channels], summed[..., channels:]], axis=2)
        return summed.reshape(EDGE, EDGE, bricks, channels)

    def over_planes(body, win, weight, planes, transposed=False):
        values = conv_rows(win, weight, planes, transposed)
        for index, plane in enumerate(planes):
            body(plane, as_plane(values[index]))

    def inside(win, weight):
        sums[...] = conv_rows(win, weight, range(EDGE), False, (1,))
        sums[: EDGE - 1] += conv_rows(win, weight, range(EDGE - 1), False, (2,))
        sums[1:] += conv_rows(win, weight, range(1, EDGE), False, (0,))

    def across(win, weight):
        sums[:1] += conv_rows(win, weight, (0,), False, (0,))
        sums[EDGE - 1 :] += conv_rows(win, weight, (EDGE - 1,), False, (2,))

    def summed_planes(body, planes):
        for plane in planes:
            body(plane, as_plane(sums[plane]))

    def rows_of(plane, index):
        return pl.ds(plane * EDGE * EDGE + index, bricks, stride=voxels)

    def scatter_plane(target, plane, values):
        for index in range(EDGE * EDGE):
            target[rows_of(plane, index), :] = values[index // EDGE, index % EDGE]

    def weight_grad(win, values, target):
        g_t[...] = values.T

        def step(dx, carry):
            pieces = [
                win[pl.ds(dx, 4), dy : dy + 4, dz : dz + 4].reshape(EDGE * plane_rows, channels)
                for dy in range(3) for dz in range(3)
            ]
            product = jnp.dot(
                g_t[...], jnp.concatenate(pieces, axis=1), preferred_element_type=F32
            )
            for tap in range(9):
                start = pl.multiple_of((dx * 9 + tap) * channels, channels)
                target[pl.ds(start, channels), :] = product[:, tap * channels : (tap + 1) * channels].T
            return carry

        lax.fori_loop(0, 3, step, 0)

    class Reduce:
        def __init__(self, refs, target):
            (self.total, self.own_t, self.other_t, self.other_win, self.send_b, self.recv_b,
             self.send_c, self.recv_c, self.own, self.kept, self.pair_sem, self.send_b_sem, self.recv_b_sem,
             self.send_c_sem, self.recv_c_sem) = refs
            self.target = target
            self.part = self.own.shape[0]
            self.half = n_dp // 2
            self.source = dp // self.half
            self.local = self.source == core
            self.flip = depth // (n_depth // 2)

        def pair_copy(self, source, target, index):
            return pltpu.make_async_remote_copy(
                src_ref=source, dst_ref=target,
                send_sem=self.pair_sem.at[2 * index], recv_sem=self.pair_sem.at[2 * index + 1],
                device_id=core_id, device_id_type=MESH,
            )

        def win_copy(self, win):
            planes = pl.ds(1 - core, EDGE + 1)
            return self.pair_copy(win.at[planes], self.other_win.at[planes], 0)

        def win_wait(self, win):
            self.win_copy(win).wait()

        def grad_copy(self):
            return self.pair_copy(self.own_t, self.other_t, 1)

        def share_grad(self, values):
            self.own_t[...] = values.T
            self.grad_copy().start()

        def rows_at(self, block, z):
            start = (block * n_depth + z) * 2 * self.part + core * (channels // 2)
            return pl.ds(pl.multiple_of(start, 8), 2 * self.part)

        def b_copy(self, t, z, side):
            target = core * self.half + t
            slot = (dp - target - 1 + n_dp) % n_dp
            return pltpu.make_async_remote_copy(
                src_ref=self.send_b.at[t, z, side], dst_ref=self.recv_b.at[slot, z],
                send_sem=self.send_b_sem.at[t, z, side], recv_sem=self.recv_b_sem.at[slot, z],
                device_id=(target, depth * 2 + side), device_id_type=MESH,
            )

        def b_arrival(self, j, z):
            return pltpu.make_async_remote_copy(
                src_ref=self.send_b.at[0, z, 0], dst_ref=self.recv_b.at[j, z],
                send_sem=self.send_b_sem.at[0, z, 0], recv_sem=self.recv_b_sem.at[j, z],
                device_id=core_id, device_id_type=MESH,
            )

        def leaves(self, t, side):
            return jnp.logical_or(dp != core * self.half + t, core != side)

        def send_chunk(self, t, z):
            block = self.total[self.rows_at(t, z), :]
            for side in range(2):
                self.send_b[t, z, side] = block[side * self.part : (side + 1) * self.part].astype(BF16)

                @pl.when(self.leaves(t, side))
                def _():
                    self.b_copy(t, z, side).start()

        def mirrored(self, index, count):
            return index + self.flip * (count - 1 - 2 * index)

        def depths(self):
            near = jnp.minimum(depth, n_depth - 1 - depth)
            order = list(range(n_depth - 1, n_depth // 2 - 1, -1))
            if n_depth == 4:
                order += [1 - near, near]
            else:
                order += list(range(n_depth // 2 - 1, -1, -1))
            return [self.mirrored(z, n_depth) for z in order]

        def multiply(self, win):
            groups = (TAPS + 1) // 4
            order = [2, 3, 5, 6, 1, 4, 0]
            depths = self.depths()
            waiting = [(t, n_depth - 1 - k) for k in range(n_depth) for t in range(self.half)]
            if n_depth == 4:
                needs = {1: (0, 2), 0: (0, 2)}
            else:
                needs = {}
            done = set()
            size = 2 * channels
            for group in order:
                corners = []
                for flip in range(2):
                    at = groups - 1 - group if flip else group
                    for side in range(2):
                        taps = [2 * at + index + side * (TAPS // 2) for index in range(2)]
                        corners.append([(tap // 9, tap // 3 % 3, tap % 3) for tap in taps])
                columns = []
                for index in range(2):
                    at = []
                    for axis in range(3):
                        a, b, c, d = (corner[index][axis] for corner in corners)
                        low = a + core * (b - a)
                        high = c + core * (d - c)
                        at.append(pl.ds(low + self.flip * (high - low), EDGE))
                    columns.append(jnp.concatenate(
                        [
                            w[tuple(at)].reshape(EDGE * plane_rows, channels)
                            for w in (win, self.other_win)
                        ],
                        axis=0,
                    ))
                both = jnp.concatenate([self.own_t[...], self.other_t[...]], axis=1)
                product = jnp.dot(
                    both, jnp.concatenate(columns, axis=1), preferred_element_type=F32
                )
                product = jnp.concatenate(
                    [product[:, :channels].T, product[:, channels:].T], axis=0
                )
                start = pl.multiple_of(self.mirrored(group, groups) * size, size)
                self.total[pl.ds(start, size), :] = product
                done.add(group)
                for t, z in list(waiting):
                    low, high = needs.get(z, (z, z + 1))
                    begin = (t * n_depth + low) * 2 * self.part
                    end = (t * n_depth + high) * 2 * self.part + channels // 2
                    if all(g in done for g in range(begin // size, -(-end // size))):
                        waiting.remove((t, z))
                        self.send_chunk(self.mirrored(t, self.half), depths[n_depth - 1 - z])

        def c_copy(self, z):
            slot = (depth - z - 1 + n_depth) % n_depth
            return pltpu.make_async_remote_copy(
                src_ref=self.send_c.at[z], dst_ref=self.recv_c.at[slot],
                send_sem=self.send_c_sem.at[z], recv_sem=self.recv_c_sem.at[slot],
                device_id=(dp, z * 2 + core), device_id_type=MESH,
            )

        def c_arrival(self, slot):
            return pltpu.make_async_remote_copy(
                src_ref=self.send_c.at[0], dst_ref=self.recv_c.at[slot],
                send_sem=self.send_c_sem.at[0], recv_sem=self.recv_c_sem.at[slot],
                device_id=core_id, device_id_type=MESH,
            )

        def forward(self, low, high):
            for z in self.depths()[low:high]:
                @pl.when(self.local)
                def _():
                    block = self.total[self.rows_at(dp - self.source * self.half, z), :]
                    self.own[...] = jnp.where(core == 0, block[: self.part], block[self.part :])

                @pl.when(jnp.logical_not(self.local))
                def _():
                    self.b_arrival(n_dp - 1, z).wait_recv()
                    self.own[...] = self.recv_b[n_dp - 1, z].astype(F32)

                for j in range(n_dp - 1):
                    self.b_arrival(j, z).wait_recv()
                summed = self.own[...]
                for j in range(n_dp - 1):
                    summed = summed + self.recv_b[j, z].astype(F32)

                @pl.when(z != depth)
                def _():
                    self.send_c[z] = summed.astype(BF16)
                    self.c_copy(z).start()

                @pl.when(z == depth)
                def _():
                    self.kept[...] = summed

        def finish(self):
            summed = self.kept[...]
            for slot in range(n_depth - 1):
                self.c_arrival(slot).wait_recv()
                summed = summed + self.recv_c[slot].astype(F32)
            self.target[...] = summed * factor

        def drain(self):
            for t in range(self.half):
                for side in range(2):
                    @pl.when(self.leaves(t, side))
                    def _():
                        for z in range(n_depth):
                            self.b_copy(t, z, side).wait_send()

            for z in range(n_depth):
                @pl.when(z != depth)
                def _():
                    self.c_copy(z).wait_send()

    if fused:
        count = len(reduce_refs) // 2
        red2 = Reduce(reduce_refs[:count], g2_ref)
        red1 = Reduce(reduce_refs[count:], g1_ref)

    def flat_of(win):
        return win[1:5, 1:5, 1:5].reshape(EDGE * plane_rows, channels)

    def first_plane(plane, values):
        values = values * occ[plane].astype(F32)
        first[plane] = values
        win_b[plane + 1, 1:5, 1:5] = (values * jax.nn.sigmoid(values)).astype(BF16)

    fill(win_a, 0, 0)
    loads[3].wait()
    inside(win_a, w1_ref)
    summed_planes(first_plane, inner)
    wait_pair(*cell_copies())
    low_key = jnp.where(
        jnp.logical_and(beside_lane, has_low), cells_low[...] - layer_key, own_key
    )
    high_key = jnp.where(
        jnp.logical_and(beside_lane, has_high), cells_high[...] + layer_key, own_key
    )

    for d in directions:
        if d[0] != 0:
            pickers[d] = picker(low_key if d[0] < 0 else high_key, *d)
    wait_pair(*halo_copies(0))
    fill(win_a, 0, 1)
    across(win_a, w1_ref)
    summed_planes(first_plane, outer)
    send_halo(1, win_b)
    if fused:
        red1.win_copy(win_a).start()
    loads[5].wait()
    loads[4].wait()
    stage_cot[...] = cot_ref[...].astype(F32)
    for plane in range(EDGE):
        cot = jnp.stack([stage_cot[rows_of(plane, index), :] for index in range(EDGE * EDGE)])
        cot = cot.reshape(EDGE, EDGE, bricks, channels)
        cot_cube[plane] = (cot * occ[plane].astype(F32)).astype(BF16)
    fill(win_b, 1, 0)
    inside(win_b, w2_ref)

    def second_plane(plane, values):
        occupancy = occ[plane].astype(F32)
        total = win_a[plane + 1, 1:5, 1:5].astype(F32) + values * occupancy
        resid[plane] = total
        gradient = (cot_cube[plane].astype(F32) * silu_slope(total)).astype(BF16)
        win_c[plane + 1, 1:5, 1:5] = gradient

    summed_planes(second_plane, inner)
    for plane in range(EDGE):
        first[plane] = silu_slope(first[plane]) * occ[plane].astype(F32)
    wait_pair(*halo_copies(1))
    fill(win_b, 1, 1)
    if fused:
        red2.win_copy(win_b).start()
    across(win_b, w2_ref)
    summed_planes(second_plane, outer)
    send_halo(2, win_c)

    if fused:
        red2.share_grad(flat_of(win_c))
    else:
        weight_grad(win_b, flat_of(win_c), g2_ref)

    def third_plane(plane, values):
        gradient = (values * first[plane]).astype(BF16)
        win_d[plane + 1, 1:5, 1:5] = gradient

    fill(win_c, 2, 0)
    over_planes(third_plane, win_c, w2_ref, inner, True)
    if fused:
        red2.win_wait(win_b)
        red2.grad_copy().wait()
        red2.multiply(win_b)
    wait_pair(*halo_copies(2))
    fill(win_c, 2, 1)
    over_planes(third_plane, win_c, w2_ref, outer, True)
    send_halo(3, win_d)
    if fused:
        red1.share_grad(flat_of(win_d))
    else:
        weight_grad(win_a, flat_of(win_d), g1_ref)

    def fourth_plane(plane, values):
        values = win_c[plane + 1, 1:5, 1:5].astype(F32) + values
        scatter_plane(stage, plane, values * occ[plane].astype(F32))

    fill(win_d, 3, 0)
    over_planes(fourth_plane, win_d, w1_ref, inner, True)
    if fused:
        red1.win_wait(win_a)
        red1.grad_copy().wait()
        red2.forward(0, 2)
        red1.multiply(win_a)
        red2.forward(2, n_depth - 1)
    for plane in range(EDGE):
        total = resid[plane]
        scatter_plane(stage_cot, plane, total * jax.nn.sigmoid(total))
    out_ref[...] = stage_cot[...].astype(BF16)
    wait_pair(*halo_copies(3))
    fill(win_d, 3, 1)
    over_planes(fourth_plane, win_d, w1_ref, outer, True)
    if fused:
        red2.forward(n_depth - 1, n_depth)
    grad_in_ref[...] = stage[...].astype(BF16)
    if fused:
        red1.forward(0, n_depth - 1)
        red2.finish()
        red1.forward(n_depth - 1, n_depth)
        red1.finish()
        red2.drain()
        red1.drain()


def writer(*refs):
    count = len(refs) // 2
    sems = refs[-1]
    copies = [
        pltpu.make_async_copy(refs[index], refs[count + index], sems.at[index])
        for index in range(count)
    ]
    for copy in copies:
        copy.start()
    for copy in copies:
        copy.wait()


def shards(n_dp, n_space, features, weight_one, weight_two, cotangent, brick_cell, voxel_mask):
    bricks, channels = features.shape[1], features.shape[3]
    factor = 1.0 / math.sqrt(n_dp * n_space * bricks * 64)
    rows = TAPS * channels
    devices = n_dp * n_space
    fused = (
        n_space % 2 == 0 and n_dp % 2 == 0 and rows % devices == 0
        and (rows // devices * 2) % 8 == 0
    )
    cube = (EDGE, EDGE, EDGE, bricks, channels)
    flat = (bricks * EDGE**3, channels)
    window = (EDGE + 2, EDGE + 2, EDGE + 2, bricks, channels)
    plane = (EDGE, EDGE, bricks, channels)
    mask = voxel_mask[0]
    scratch = [
        pltpu.VMEM(flat, BF16), pltpu.VMEM(flat, BF16),
        pltpu.VMEM(mask.shape, jnp.int32), pltpu.VMEM(brick_cell.shape, jnp.int32),
        pltpu.VMEM(weight_one.shape, BF16), pltpu.VMEM(weight_two.shape, BF16),
        pltpu.SemaphoreType.DMA((6,)),
        pltpu.VMEM(window, BF16), pltpu.VMEM(window, BF16),
        pltpu.VMEM(window, BF16), pltpu.VMEM(window, BF16),
        pltpu.VMEM(cube, F32), pltpu.VMEM(cube, F32),
        pltpu.VMEM((EDGE, 8 * bricks, 2 * channels), F32),
        pltpu.VMEM(cube, BF16), pltpu.VMEM(cube, BF16),
        pltpu.VMEM(flat, F32), pltpu.VMEM(flat, F32),
        pltpu.VMEM((channels, flat[0]), BF16),
        pltpu.VMEM((4,) + plane, BF16), pltpu.VMEM((4,) + plane, BF16),
        pltpu.VMEM((4,) + plane, BF16), pltpu.VMEM((4,) + plane, BF16),
        pltpu.VMEM((8, 128), F32), pltpu.VMEM((8, 128), F32), pltpu.VMEM((8, 128), F32),
        pltpu.SemaphoreType.DMA((4, 2)), pltpu.SemaphoreType.DMA((4, 2)),
        pltpu.SemaphoreType.DMA((4,)),
    ]
    if fused:
        part = rows // devices
        n_depth = n_space // 2
        half = n_dp // 2
        for _ in range(2):
            scratch += [
                pltpu.VMEM(((TAPS + 1) // 2 * channels, channels), F32),
                pltpu.VMEM((channels, flat[0]), BF16), pltpu.VMEM((channels, flat[0]), BF16),
                pltpu.VMEM(window, BF16),
                pltpu.VMEM((half, n_depth, 2, part, channels), BF16),
                pltpu.VMEM((n_dp, n_depth, part, channels), BF16),
                pltpu.VMEM((n_depth, part, channels), BF16),
                pltpu.VMEM((n_depth - 1, part, channels), BF16),
                pltpu.VMEM((part, channels), F32),
                pltpu.VMEM((part, channels), F32),
                pltpu.SemaphoreType.DMA((4,)),
                pltpu.SemaphoreType.DMA((half, n_depth, 2)),
                pltpu.SemaphoreType.DMA((n_dp, n_depth)),
                pltpu.SemaphoreType.DMA((n_depth,)),
                pltpu.SemaphoreType.DMA((n_depth - 1,)),
            ]
        grad_shape = (part, channels)
    else:
        grad_shape = (rows, channels)
    vmem = pl.BlockSpec(memory_space=pltpu.VMEM)
    hbm = pl.BlockSpec(memory_space=pltpu.HBM)
    results = pl.pallas_call(
        functools.partial(kernel, n_dp, n_space, fused, factor),
        out_shape=(
            jax.ShapeDtypeStruct(flat, BF16), jax.ShapeDtypeStruct(flat, BF16),
            jax.ShapeDtypeStruct(grad_shape, F32), jax.ShapeDtypeStruct(grad_shape, F32),
        ),
        in_specs=[hbm] * 6,
        out_specs=(vmem,) * 4,
        scratch_shapes=scratch,
        compiler_params=pltpu.CompilerParams(
            collective_id=0, has_side_effects=True, vmem_limit_bytes=VMEM_LIMIT
        ),
    )(*(
        pltpu.with_memory_space_constraint(argument, pltpu.HBM)
        for argument in (
            features.reshape(flat), cotangent.reshape(flat), mask, brick_cell,
            weight_one, weight_two,
        )
    ))

    if fused:
        results = pl.pallas_call(
            writer,
            out_shape=tuple(jax.ShapeDtypeStruct(r.shape, r.dtype) for r in results),
            in_specs=[vmem] * 4,
            out_specs=(hbm,) * 4,
            scratch_shapes=[pltpu.SemaphoreType.DMA((4,))],
            compiler_params=pltpu.CompilerParams(vmem_limit_bytes=1024 * 1024),
        )(*results)
    block_out, input_grad, grad_one, grad_two = results
    grad_one, grad_two = grad_one.reshape(-1), grad_two.reshape(-1)
    if not fused:
        grad_one, grad_two = (
            lax.psum_scatter(g, ("dp", "space"), scatter_dimension=0, tiled=True) * factor
            for g in (grad_one, grad_two)
        )
    shape = features.shape
    return (block_out.reshape(shape), input_grad.reshape(shape), grad_one, grad_two)


def solution(mesh):
    return jax.shard_map(
        functools.partial(shards, mesh.shape["dp"], mesh.shape["space"]),
        mesh=mesh,
        in_specs=(
            P("dp", "space", None, None),
            P(),
            P(),
            P("dp", "space", None, None),
            P("dp", "space"),
            P("dp", "space", None),
        ),
        out_specs=(
            P("dp", "space", None, None),
            P("dp", "space", None, None),
            P(("dp", "space")),
            P(("dp", "space")),
        ),
        check_vma=False,
    )
```
